128 devices in a mesh: req: 8 (over x, y_hi), hid: 16 (over y_lo, z, core).
Axes of the slice: x: 4, y: 4 (y_hi: 2, y_lo: 2; y = y_hi * 2 + y_lo), z: 4, core: 2. Of those that a mesh axis runs over, the one named last changes fastest.
Arguments:
- input_activations: bfloat16 [8, 512, 4096], P('req'), may hold values from -6 to 6
- prompt_extents: int32 [8], P('req'), may hold values from 1 to 512, as said below
- continuing_flags: int32 [8], P('req'), may hold values from 0 to 1, as said below
- owning_index: int32 [8], P('req'), may hold values from 0 to 15
- partition_arrangement: int32 [128], replicated, may hold values from 0 to 127, each once
- training_accept_pieces: float32 [4096, 4096], P(('req', 'hid')), may hold values from -0.09375 to 0.09375
- training_lookup_pieces: float32 [4096, 4096], P(('req', 'hid')), may hold values from -0.09375 to 0.09375
- training_content_pieces: float32 [4096, 4096], P(('req', 'hid')), may hold values from -0.09375 to 0.09375
- normalizer_scales: bfloat16 [2, 4096], replicated, may hold values from 0.5 to 1.5
- prior_step_blends: bfloat16 [7, 4096], replicated, may hold values from 0.049804688 to 0.94921875
- forgetting_bias_vector: float32 [4096], P('hid'), may hold values from -7 to -3
- forgetting_left_lowrank: bfloat16 [4096, 128], replicated, may hold values from -0.09375 to 0.09375
- forgetting_right_lowrank: bfloat16 [128, 4096], P(None, 'hid'), may hold values from -0.5 to 0.5
- instant_emphasis: float32 [4096], P('hid'), may hold values from -3 to 3
- group_normalizer_scale: float32 [4096], P('hid'), may hold values from 0.5 to 1.5
- gating_projection: bfloat16 [4096, 4096], P(None, 'hid'), may hold values from -0.09375 to 0.09375
- mixing_exit_projection: bfloat16 [4096, 4096], P('hid'), may hold values from -0.09375 to 0.09375
- kept_summary_places: float32 [8, 16, 64, 64, 64], P('req', 'hid'), may hold values from -6 to 6
- previous_normed_entries: bfloat16 [8, 2, 4096], P('req'), may hold values from -6 to 6
- feedforward_entry_proj: bfloat16 [14336, 4096], P(('req', 'hid')), may hold values from -0.09375 to 0.09375
- feedforward_exit_proj: bfloat16 [14336, 4096], P(('req', 'hid')), may hold values from -0.046875 to 0.046875
- feedforward_accept_proj: bfloat16 [4096, 4096], P(None, 'hid'), may hold values from -0.09375 to 0.09375
Outputs:
- layer_out: bfloat16 [8, 512, 4096], P('req', None, 'hid')
- new_states: float32 [8, 64, 64, 64], P('req', 'hid')
- new_shift: bfloat16 [8, 2, 4096], P('req')
The draws below stay inside these ranges and needn't reach their ends.
Inputs may be any that keep to these rules, and one draw needn't show every extreme that they name: `prompt_extents`: in every draw some request has length 512. `continuing_flags`: at least one request has 1 and at least one has 0. `owning_index`: read only where continuing_flags is 1. `partition_arrangement`: each of 0 to 127 appears once.
All inputs are finite; a program needn't handle non-finite values.
Results may differ from the reference program's by a relative error of at most 0.02.
Values may be sent and summed in bfloat16 or wider, within the bound.
A program may use at most 192 MiB of HBM per device.

```python
from functools import partial
import jax
import jax.numpy as jnp
from jax import lax

EMBEDDING_DIM = 4096
ATTENTION_GROUPS = 64
GROUP_DIMENSION = 64
FF = 14336
RANK = 128
L = 512
REQS = 8
HOLDERS = 16
SHARDS = 128
BLK = 64
N_REQ = 8
N_HID = 16


def draw_prompt_extents(key, part):
    first_key, second_key = jax.random.split(jax.random.fold_in(key, 11))
    values = jax.random.randint(first_key, (REQS,), 1, L + 1)
    chosen = jax.random.randint(second_key, (), 0, REQS)
    return jnp.where(jnp.arange(REQS) == chosen, L, values).astype(jnp.int32)


def draw_continuing_flags(key, part):
    bits_key, first_key, second_key = jax.random.split(jax.random.fold_in(key, 37), 3)
    values = jax.random.randint(bits_key, (REQS,), 0, 2)
    forced_one = jax.random.randint(first_key, (), 0, REQS)
    forced_zero = (forced_one + 1 + jax.random.randint(second_key, (), 0, REQS - 1)) % REQS
    places = jnp.arange(REQS)
    values = jnp.where(places == forced_one, 1, values)
    values = jnp.where(places == forced_zero, 0, values)
    return values.astype(jnp.int32)


def touch_ends(array, own_key, smallest, top_value):
    spot = [jax.random.randint(jax.random.fold_in(own_key, axis), (), 0, length) for axis, length in enumerate(array.shape)]
    widest = array.shape.index(max(array.shape))
    neighbour = spot[:widest] + [(spot[widest] + 1) % array.shape[widest]] + spot[widest + 1:]
    return array.at[tuple(spot)].set(smallest).at[tuple(neighbour)].set(top_value)


def level_of(rng, dims, cuts, smallest, top_value):
    level = 1.0
    for dim, blocks in cuts:
        draws = jax.random.uniform(jax.random.fold_in(jax.random.fold_in(rng, 6), dim), (blocks,), jnp.float32, smallest / len(cuts), top_value / len(cuts))
        level = level * jnp.repeat(jnp.exp(draws), dims[dim] // blocks).reshape((-1,) + (1,) * (len(dims) - 1 - dim))
    return level


def gaussian(own_key, dims, scale, reach, cuts=(), dtype=jnp.bfloat16):
    level = level_of(own_key, dims, cuts, -0.22, 0.18) if cuts else 1.0
    entries = jax.random.normal(own_key, dims, jnp.float32) * scale * level
    return jnp.minimum(jnp.maximum(entries, -reach), reach).astype(dtype)


def setup_inputs(seed: int = 0) -> dict:
    arg_keys = jax.random.split(jax.random.key(seed), 23)
    return {
        "input_activations": gaussian(arg_keys[0], (REQS, L, EMBEDDING_DIM), 1.0, 6.0, ((0, 8),)),
        "prompt_extents": draw_prompt_extents(jax.random.fold_in(arg_keys[22], 71), 0),
        "continuing_flags": draw_continuing_flags(jax.random.fold_in(arg_keys[22], 71), 0),
        "owning_index": touch_ends(jax.random.randint(arg_keys[3], (REQS,), 0, HOLDERS), jax.random.fold_in(arg_keys[3], 1), 0, HOLDERS - 1).astype(jnp.int32),
        "partition_arrangement": jax.random.permutation(arg_keys[4], SHARDS).astype(jnp.int32),
        "training_accept_pieces": gaussian(arg_keys[5], (EMBEDDING_DIM, EMBEDDING_DIM), EMBEDDING_DIM ** -0.5, 0.09375, ((0, 128),), jnp.float32),
        "training_lookup_pieces": gaussian(arg_keys[6], (EMBEDDING_DIM, EMBEDDING_DIM), EMBEDDING_DIM ** -0.5, 0.09375, ((0, 128),), jnp.float32),
        "training_content_pieces": gaussian(arg_keys[7], (EMBEDDING_DIM, EMBEDDING_DIM), EMBEDDING_DIM ** -0.5, 0.09375, ((0, 128),), jnp.float32),
        "normalizer_scales": jnp.clip(1.0 + 0.1 * jax.random.normal(arg_keys[8], (2, EMBEDDING_DIM), jnp.float32), 0.5, 1.5).astype(jnp.bfloat16),
        "prior_step_blends": jnp.clip(jax.random.uniform(arg_keys[9], (7, EMBEDDING_DIM), jnp.float32, 0.049804688, 0.94921875), 0.049804688, 0.94921875).astype(jnp.bfloat16),
        "forgetting_bias_vector": jnp.clip(-7.0 + 4.0 * jax.random.uniform(arg_keys[10], (EMBEDDING_DIM,), jnp.float32) ** level_of(arg_keys[10], (EMBEDDING_DIM,), ((0, 16),), -0.2, 0.2), -7.0, -3.0),
        "forgetting_left_lowrank": gaussian(arg_keys[11], (EMBEDDING_DIM, RANK), EMBEDDING_DIM ** -0.5, 0.09375),
        "forgetting_right_lowrank": gaussian(arg_keys[12], (RANK, EMBEDDING_DIM), RANK ** -0.5, 0.5, ((1, 16),)),
        "instant_emphasis": gaussian(arg_keys[13], (EMBEDDING_DIM,), 0.5, 3.0, ((0, 16),), jnp.float32),
        "group_normalizer_scale": jnp.clip(1.0 + 0.1 * jax.random.normal(arg_keys[14], (EMBEDDING_DIM,), jnp.float32), 0.5, 1.5),
        "gating_projection": gaussian(arg_keys[15], (EMBEDDING_DIM, EMBEDDING_DIM), EMBEDDING_DIM ** -0.5, 0.09375, ((1, 16),)),
        "mixing_exit_projection": gaussian(arg_keys[16], (EMBEDDING_DIM, EMBEDDING_DIM), EMBEDDING_DIM ** -0.5, 0.09375, ((0, 16),)),
        "kept_summary_places": gaussian(arg_keys[17], (REQS, HOLDERS, ATTENTION_GROUPS, GROUP_DIMENSION, GROUP_DIMENSION), 1.0, 6.0, ((0, 8), (1, 16)), jnp.float32),
        "previous_normed_entries": gaussian(arg_keys[18], (REQS, 2, EMBEDDING_DIM), 1.0, 6.0, ((0, 8),)),
        "feedforward_entry_proj": gaussian(arg_keys[19], (FF, EMBEDDING_DIM), EMBEDDING_DIM ** -0.5, 0.09375, ((0, 128),)),
        "feedforward_exit_proj": gaussian(arg_keys[20], (FF, EMBEDDING_DIM), FF ** -0.5, 0.046875, ((0, 128),)),
        "feedforward_accept_proj": gaussian(arg_keys[21], (EMBEDDING_DIM, EMBEDDING_DIM), EMBEDDING_DIM ** -0.5, 0.09375, ((1, 16),)),
    }


def layer_norm(values, gain):
    center = values - lax.optimization_barrier(jnp.mean(values, axis=-1, keepdims=True))
    spread = lax.optimization_barrier(jnp.mean(center * center, axis=-1, keepdims=True))
    return center / jnp.sqrt(spread + 1e-05) * gain

def head_norm(outputs, gain_rows):
    center = outputs - lax.optimization_barrier(jnp.mean(outputs, axis=-1, keepdims=True))
    spread = lax.optimization_barrier(jnp.mean(center * center, axis=-1, keepdims=True))
    return center / jnp.sqrt(spread + 0.00064) * gain_rows

def shifted(values, first_row):
    return jnp.concatenate([first_row[None, :], values[:-1]], axis=0)

def rounded(values):
    return lax.optimization_barrier(values.astype(jnp.bfloat16)).astype(jnp.float32)

def segment_step(extra_diagonal_term, carried_summary, piece_sequence):
    acceptance_vectors, present_lookup_vectors, content_vectors, decays = piece_sequence
    inclusive = jnp.cumsum(decays, axis=0)
    exclusive = inclusive - decays
    closing = inclusive[-1]
    resulting_activations = jnp.einsum('thi,hij->thj', acceptance_vectors * jnp.exp(exclusive), carried_summary, precision=lax.Precision.HIGHEST)
    distance = exclusive[:, None] - inclusive[None, :]
    sizing = decays.shape[0]
    earlier = (jnp.arange(sizing)[:, None] > jnp.arange(sizing)[None, :]).astype(jnp.float32)
    factor = jnp.exp(jnp.minimum(distance, 0.0)) * earlier[:, :, None, None]
    scores = lax.optimization_barrier(jnp.sum(acceptance_vectors[:, None] * factor * present_lookup_vectors[None, :], axis=-1))
    resulting_activations = resulting_activations + jnp.einsum('tsh,shj->thj', scores, content_vectors, precision=lax.Precision.HIGHEST)
    resulting_activations = resulting_activations + lax.optimization_barrier(jnp.sum(acceptance_vectors * extra_diagonal_term * present_lookup_vectors, axis=-1, keepdims=True)) * content_vectors
    weighted = present_lookup_vectors * jnp.exp(closing[None] - inclusive)
    carried_summary = jnp.exp(closing)[:, :, None] * carried_summary + jnp.einsum('shi,shj->hij', weighted, content_vectors, precision=lax.Precision.HIGHEST)
    return (carried_summary, resulting_activations)

def reference(input_activations, prompt_extents, continuing_flags, owning_index, partition_arrangement, training_accept_pieces, training_lookup_pieces, training_content_pieces, normalizer_scales, prior_step_blends, forgetting_bias_vector, forgetting_left_lowrank, forgetting_right_lowrank, instant_emphasis, group_normalizer_scale, gating_projection, mixing_exit_projection, kept_summary_places, previous_normed_entries, feedforward_entry_proj, feedforward_exit_proj, feedforward_accept_proj):
    shard_rows = EMBEDDING_DIM // SHARDS
    server = rounded(jnp.stack([training_accept_pieces, training_lookup_pieces, training_content_pieces]))
    gain_rows = normalizer_scales.astype(jnp.float32)
    mix_rows = prior_step_blends.astype(jnp.float32)
    out_blocks = mixing_exit_projection.astype(jnp.float32).reshape(N_HID, EMBEDDING_DIM // N_HID, EMBEDDING_DIM)
    value_sets = feedforward_exit_proj.astype(jnp.float32).reshape(N_REQ, N_HID, FF // SHARDS, EMBEDDING_DIM)
    key_table = feedforward_entry_proj.astype(jnp.float32)
    recept_table = feedforward_accept_proj.astype(jnp.float32)
    positions = jnp.arange(L)
    segment_cursor = partial(segment_step, instant_emphasis.reshape(ATTENTION_GROUPS, GROUP_DIMENSION))

    def by_blocks(values):
        return values.reshape(L // BLK, BLK, ATTENTION_GROUPS, GROUP_DIMENSION)

    def per_request(inputs):
        token_rows, length, resuming, slot, saved, carry_rows = inputs
        present = positions < length
        carried = carry_rows.astype(jnp.float32)
        normed_in = layer_norm(token_rows.astype(jnp.float32), gain_rows[0])
        before = shifted(normed_in, jnp.where(resuming == 1, carried[0], 0.0))
        blended = (normed_in[None] + (before - normed_in)[None] * mix_rows[:5, None, :]).astype(jnp.bfloat16)
        permuted = jnp.take(blended[:3].reshape(3, L, SHARDS, shard_rows), partition_arrangement, axis=2).reshape(3, L, EMBEDDING_DIM)
        projected = jnp.einsum('mtd,mdc->mtc', permuted.astype(jnp.float32), server, precision=lax.Precision.HIGHEST)
        low_rank = jnp.tanh(jnp.dot(blended[3], forgetting_left_lowrank, preferred_element_type=jnp.float32)).astype(jnp.bfloat16)
        log_decay = -jnp.exp(forgetting_bias_vector + jnp.dot(low_rank, forgetting_right_lowrank, preferred_element_type=jnp.float32))
        log_decay = jnp.where(present[:, None], log_decay, 0.0)
        gate = jax.nn.silu(jnp.dot(blended[4], gating_projection, preferred_element_type=jnp.float32))
        present_lookup_vectors = jnp.where(present[:, None], projected[1], 0.0)
        carried_summary = jnp.where(resuming == 1, lax.dynamic_index_in_dim(saved, slot, 0, keepdims=False), 0.0)
        carried_summary, outputs = lax.scan(segment_cursor, carried_summary, (by_blocks(projected[0]), by_blocks(present_lookup_vectors), by_blocks(projected[2]), by_blocks(log_decay)))
        grouped = head_norm(outputs.reshape(L, ATTENTION_GROUPS, GROUP_DIMENSION), group_normalizer_scale.reshape(ATTENTION_GROUPS, GROUP_DIMENSION)).reshape(L, EMBEDDING_DIM)
        gated = (grouped * gate).astype(jnp.bfloat16)
        head_sets = gated.astype(jnp.float32).reshape(L, N_HID, EMBEDDING_DIM // N_HID)
        partials = jnp.einsum('lnc,ncd->nld', head_sets, out_blocks, precision=lax.Precision.HIGHEST)
        attended = lax.optimization_barrier(jnp.sum(rounded(partials), axis=0))
        middle = (token_rows.astype(jnp.float32) + attended).astype(jnp.bfloat16)
        chan_in = layer_norm(middle.astype(jnp.float32), gain_rows[1])
        chan_before = shifted(chan_in, jnp.where(resuming == 1, carried[1], 0.0))
        chan_mixed = (chan_in[None] + (chan_before - chan_in)[None] * mix_rows[5:, None, :]).astype(jnp.bfloat16)
        inner = jnp.dot(chan_mixed[0].astype(jnp.float32), key_table.T, precision=lax.Precision.HIGHEST)
        hidden = jnp.square(jnp.maximum(inner, 0.0)).astype(jnp.bfloat16)
        partial_sets = jnp.einsum('lgnu,gnud->nld', hidden.astype(jnp.float32).reshape(L, N_REQ, N_HID, FF // SHARDS), value_sets, precision=lax.Precision.HIGHEST)
        summed = lax.optimization_barrier(jnp.sum(rounded(partial_sets), axis=0))
        gate_rows = jax.nn.sigmoid(jnp.dot(chan_mixed[1].astype(jnp.float32), recept_table, precision=lax.Precision.HIGHEST))
        combined = middle.astype(jnp.float32) + gate_rows * summed
        layer_row = jnp.where(present[:, None], combined, 0.0).astype(jnp.bfloat16)
        last_index = length - 1
        shift_out = jnp.stack([lax.dynamic_index_in_dim(normed_in, last_index, 0, keepdims=False), lax.dynamic_index_in_dim(chan_in, last_index, 0, keepdims=False)]).astype(jnp.bfloat16)
        return (layer_row, carried_summary, shift_out)
    layer_out, new_states, new_shift = lax.map(per_request, (input_activations, prompt_extents, continuing_flags, owning_index, kept_summary_places, previous_normed_entries))
    return (layer_out, new_states, new_shift)
```

```python
from functools import partial

import jax
import jax.numpy as jnp
from jax import lax
from jax.experimental import pallas as pl
from jax.experimental.pallas import tpu as pltpu
from jax.sharding import PartitionSpec as P

HEAD = 64
CHUNK = 16
TILE = 64
PAIR = 128
KC = 512
VMEM_LIMIT = 58 * 1024 * 1024
F32 = jnp.float32
BF16 = jnp.bfloat16
VM = pl.BlockSpec(memory_space=pltpu.VMEM)
SM = pl.BlockSpec(memory_space=pltpu.SMEM)
HB = pl.BlockSpec(memory_space=pl.ANY)


def nt_dot(a, b):
    return lax.dot_general(a, b, (((1,), (1,)), ((), ())), preferred_element_type=F32)


def tn_dot(a, b):
    return lax.dot_general(a, b, (((0,), (0,)), ((), ())), preferred_element_type=F32)


def nn_dot(a, b):
    return jnp.dot(a, b, preferred_element_type=F32)


def row_stats(x_ref, eps):
    rows, width = x_ref.shape

    def add_sum(c, total):
        part = x_ref[:, pl.ds(pl.multiple_of(c * KC, KC), KC)].astype(F32)
        return total + jnp.sum(part, axis=1, keepdims=True)

    def add_square(c, total):
        part = x_ref[:, pl.ds(pl.multiple_of(c * KC, KC), KC)].astype(F32) - mean
        return total + jnp.sum(part * part, axis=1, keepdims=True)

    zero = jnp.zeros((rows, 1), F32)
    mean = lax.fori_loop(0, width // KC, add_sum, zero) / width
    var = lax.fori_loop(0, width // KC, add_square, zero) / width
    return mean, 1.0 / jnp.sqrt(var + eps)


def normed_and_delta(x_ref, first_ref, gain_ref, which, cols, mean, inv):
    part = x_ref[:, cols].astype(F32)
    normed = (part - mean) * inv * gain_ref[:, cols].astype(F32)[which : which + 1]
    before = pltpu.roll(normed, 1, 0)
    row = lax.broadcasted_iota(jnp.int32, normed.shape, 0)
    before = jnp.where(row == 0, first_ref[:, cols], before)
    return normed, before - normed


def time_mix_kernel(
    perm_ref, len_ref, x_ref, first_ref, gain_ref, mix_ref, w_ref, gating_ref, left_ref,
    right_ref, bias_ref, bonus_ref, gscale_ref, s0_ref, exit_ref,
    terms_ref, state_ref,
    w_scr, acc, acc_low, acc_gate, logw_scr, prod_scr, gated_scr, st_scr, sem,
):
    rows, width = x_ref.shape
    blocks = w_scr.shape[0]
    block_rows = w_scr.shape[1]
    lw = acc_gate.shape[1]

    def start(j, carry):
        pltpu.make_async_copy(w_ref.at[j], w_scr.at[perm_ref[j]], sem).start()
        return carry

    lax.fori_loop(0, blocks, start, 0)
    mean, inv = row_stats(x_ref, 1e-05)
    acc[...] = jnp.zeros_like(acc)
    acc_low[...] = jnp.zeros_like(acc_low)
    acc_gate[...] = jnp.zeros_like(acc_gate)
    pltpu.make_async_copy(w_ref, w_scr, sem).wait()
    per = KC // block_rows

    def project(c, carry):
        cols = pl.ds(pl.multiple_of(c * KC, KC), KC)
        normed, delta = normed_and_delta(x_ref, first_ref, gain_ref, 0, cols, mean, inv)
        mix = mix_ref[:, cols].astype(F32)

        def blend(m):
            return (normed + delta * mix[m : m + 1]).astype(BF16)

        for m in range(3):
            wm = w_scr[pl.ds(c * per, per), :, m * lw : (m + 1) * lw].reshape(KC, lw)
            acc[:, m * lw : (m + 1) * lw] += nn_dot(blend(m), wm)
        acc_low[...] += nn_dot(blend(3), left_ref[cols, :])
        acc_gate[...] += nn_dot(blend(4), gating_ref[cols, :])
        return carry

    lax.fori_loop(0, width // KC, project, 0)
    length = len_ref[0]
    present = lax.broadcasted_iota(jnp.int32, (rows, lw), 0) < length
    low = jnp.tanh(acc_low[...]).astype(BF16)
    log_decay = -jnp.exp(bias_ref[...] + nn_dot(low, right_ref[...]))
    logw_scr[...] = jnp.where(present, log_decay, 0.0)
    acc[:, lw : 2 * lw] = jnp.where(present, acc[:, lw : 2 * lw], 0.0)

    pairs = lw // PAIR
    hole = jnp.zeros((HEAD, HEAD), F32)
    for p in range(pairs):
        top = jnp.concatenate([s0_ref[2 * p], hole], axis=1)
        bottom = jnp.concatenate([hole, s0_ref[2 * p + 1]], axis=1)
        st_scr[p] = jnp.concatenate([top, bottom], axis=0).T

    def same_head(size):
        a = lax.broadcasted_iota(jnp.int32, (size, size), 0) // HEAD
        b = lax.broadcasted_iota(jnp.int32, (size, size), 1) // HEAD
        return a == b

    ones = jnp.where(same_head(lw), 1.0, 0.0).astype(BF16)
    pair_mask = same_head(PAIR)
    slot = lax.broadcasted_iota(jnp.int32, (TILE, lw), 0) % CHUNK

    def head_sum(values):
        high = values.astype(BF16)
        rest = (values - high.astype(F32)).astype(BF16)
        return nn_dot(high, ones) + nn_dot(rest, ones)

    def tile_step(t, carry):
        here = pl.ds(pl.multiple_of(t * TILE, TILE), TILE)
        r = acc[here, 0:lw]
        k = acc[here, lw : 2 * lw]
        v = acc[here, 2 * lw : 3 * lw]
        decay = logw_scr[here, :]
        incl = decay
        step = 1
        while step < CHUNK:
            incl = incl + jnp.where(slot >= step, pltpu.roll(incl, step, 0), 0.0)
            step *= 2
        excl = incl - decay
        prod_scr[0:TILE, :] = (r * bonus_ref[...] * k).astype(BF16)
        for d in range(1, CHUNK):
            gap = jnp.minimum(excl - pltpu.roll(incl, d, 0), 0.0)
            term = jnp.where(slot >= d, r * pltpu.roll(k, d, 0) * jnp.exp(gap), 0.0)
            prod_scr[d * TILE : (d + 1) * TILE, :] = term.astype(BF16)
        scores = nn_dot(prod_scr[...], ones)
        out = scores[0:TILE] * v
        for d in range(1, CHUNK):
            out = out + scores[d * TILE : (d + 1) * TILE] * pltpu.roll(v, d, 0)
        rw = (r * jnp.exp(excl)).astype(BF16)
        vb = v.astype(BF16)
        pieces = []
        for c in range(TILE // CHUNK):
            lo, hi = c * CHUNK, (c + 1) * CHUNK
            closing = incl[hi - 1 : hi]
            kw = (k[lo:hi] * jnp.exp(closing - incl[lo:hi])).astype(BF16)
            fade = jnp.exp(closing)
            parts = []
            for p in range(pairs):
                a, b = p * PAIR, (p + 1) * PAIR
                st = st_scr[p]
                parts.append(nt_dot(rw[lo:hi, a:b], st.astype(BF16)))
                grown = tn_dot(vb[lo:hi, a:b], kw[:, a:b])
                st_scr[p] = st * fade[:, a:b] + jnp.where(pair_mask, grown, 0.0)
            pieces.append(jnp.concatenate(parts, axis=1))
        out = out + jnp.concatenate(pieces, axis=0)
        center = out - head_sum(out) * (1.0 / HEAD)
        spread = head_sum(center * center) * (1.0 / HEAD)
        grouped = center / jnp.sqrt(spread + 0.00064) * gscale_ref[...]
        g = acc_gate[here, :]
        gate = g / (1.0 + jnp.exp(-g))
        gated_scr[here, :] = (grouped * gate).astype(BF16)
        return carry

    lax.fori_loop(0, rows // TILE, tile_step, 0)
    for p in range(pairs):
        full = st_scr[p].T
        state_ref[2 * p] = full[0:HEAD, 0:HEAD]
        state_ref[2 * p + 1] = full[HEAD:PAIR, HEAD:PAIR]

    def leave(c, carry):
        cols = pl.ds(pl.multiple_of(c * KC, KC), KC)
        terms_ref[:, cols] = nn_dot(gated_scr[...], exit_ref[:, cols]).astype(BF16)
        return carry

    lax.fori_loop(0, width // KC, leave, 0)


def time_mix(perm, length, x, first, gains, mixes, w, gating, left, right, bias, bonus, gscale, s0, exit_w):
    rows, width = x.shape
    lw = gating.shape[1]
    return pl.pallas_call(
        time_mix_kernel,
        out_shape=(
            jax.ShapeDtypeStruct((rows, width), BF16),
            jax.ShapeDtypeStruct(s0.shape, F32),
        ),
        in_specs=[SM, SM, VM, VM, VM, VM, HB] + [VM] * 8,
        out_specs=(VM, VM),
        scratch_shapes=[
            pltpu.VMEM(w.shape, BF16),
            pltpu.VMEM((rows, 3 * lw), F32),
            pltpu.VMEM((rows, left.shape[1]), F32),
            pltpu.VMEM((rows, lw), F32),
            pltpu.VMEM((rows, lw), F32),
            pltpu.VMEM((CHUNK * TILE, lw), BF16),
            pltpu.VMEM((rows, lw), BF16),
            pltpu.VMEM((lw // PAIR, PAIR, PAIR), F32),
            pltpu.SemaphoreType.DMA,
        ],
        compiler_params=pltpu.CompilerParams(vmem_limit_bytes=VMEM_LIMIT),
        name="time_mix",
    )(perm, length, x, first, gains, mixes, w, gating, left, right, bias, bonus, gscale, s0, exit_w)


def channel_mix_kernel(
    x_ref, first_ref, gain_ref, mix_ref, accept_ref, key_ref, value_ref,
    terms_ref, gate_ref,
    key_scr, value_scr, inner, acc_gate, hidden, sems,
):
    width = x_ref.shape[1]
    key_copy = pltpu.make_async_copy(key_ref, key_scr, sems.at[0])
    value_copy = pltpu.make_async_copy(value_ref, value_scr, sems.at[1])
    key_copy.start()
    value_copy.start()
    mean, inv = row_stats(x_ref, 1e-05)
    inner[...] = jnp.zeros_like(inner)
    acc_gate[...] = jnp.zeros_like(acc_gate)
    key_copy.wait()

    def project(c, carry):
        cols = pl.ds(pl.multiple_of(c * KC, KC), KC)
        normed, delta = normed_and_delta(x_ref, first_ref, gain_ref, 1, cols, mean, inv)
        mix = mix_ref[:, cols].astype(F32)
        inner[...] += nt_dot((normed + delta * mix[5:6]).astype(BF16), key_scr[:, cols])
        acc_gate[...] += nn_dot((normed + delta * mix[6:7]).astype(BF16), accept_ref[cols, :])
        return carry

    lax.fori_loop(0, width // KC, project, 0)
    positive = jnp.maximum(inner[...], 0.0)
    hidden[...] = (positive * positive).astype(BF16)
    gate_ref[...] = jax.nn.sigmoid(acc_gate[...])
    value_copy.wait()

    def leave(c, carry):
        cols = pl.ds(pl.multiple_of(c * KC, KC), KC)
        terms_ref[:, cols] = nn_dot(hidden[...], value_scr[:, cols]).astype(BF16)
        return carry

    lax.fori_loop(0, width // KC, leave, 0)


def channel_mix(x, first, gains, mixes, accept, key_rows, value_rows):
    rows, width = x.shape
    lw = accept.shape[1]
    units = key_rows.shape[0]
    return pl.pallas_call(
        channel_mix_kernel,
        out_shape=(
            jax.ShapeDtypeStruct((rows, width), BF16),
            jax.ShapeDtypeStruct((rows, lw), F32),
        ),
        in_specs=[VM] * 5 + [HB] * 2,
        out_specs=(VM, VM),
        scratch_shapes=[
            pltpu.VMEM(key_rows.shape, BF16),
            pltpu.VMEM(value_rows.shape, BF16),
            pltpu.VMEM((rows, units), F32),
            pltpu.VMEM((rows, lw), F32),
            pltpu.VMEM((rows, units), BF16),
            pltpu.SemaphoreType.DMA((2,)),
        ],
        compiler_params=pltpu.CompilerParams(vmem_limit_bytes=VMEM_LIMIT),
        name="channel_mix",
    )(x, first, gains, mixes, accept, key_rows, value_rows)


def norm_row(row, gain):
    center = row - jnp.mean(row)
    return center / jnp.sqrt(jnp.mean(center * center) + 1e-05) * gain


def local(
    input_activations,
    prompt_extents,
    continuing_flags,
    owning_index,
    partition_arrangement,
    training_accept_pieces,
    training_lookup_pieces,
    training_content_pieces,
    normalizer_scales,
    prior_step_blends,
    forgetting_bias_vector,
    forgetting_left_lowrank,
    forgetting_right_lowrank,
    instant_emphasis,
    group_normalizer_scale,
    gating_projection,
    mixing_exit_projection,
    kept_summary_places,
    previous_normed_entries,
    feedforward_entry_proj,
    feedforward_exit_proj,
    feedforward_accept_proj,
):
    x = input_activations[0]
    rows, width = x.shape
    lw = mixing_exit_projection.shape[0]
    hid = lax.axis_size("hid")
    block_rows = training_accept_pieces.shape[0]
    length = prompt_extents[0]
    resuming = continuing_flags[0]
    gains = normalizer_scales.astype(F32)
    carried = jnp.where(resuming == 1, previous_normed_entries[0].astype(F32), 0.0)

    own = jnp.stack([training_accept_pieces, training_lookup_pieces, training_content_pieces])
    own = own.astype(BF16).reshape(3, block_rows, hid, lw).transpose(2, 1, 0, 3)
    own = own.reshape(hid, block_rows, 3 * lw)
    swapped = lax.all_to_all(own, "hid", split_axis=0, concat_axis=0, tiled=True)
    fetched = lax.all_to_all(
        kept_summary_places[0, 0].astype(BF16).reshape(hid, -1, HEAD, HEAD),
        "hid", split_axis=0, concat_axis=0, tiled=True,
    )
    chosen = lax.dynamic_index_in_dim(fetched, owning_index[0], 0, keepdims=False)
    s0 = jnp.where(resuming == 1, chosen.astype(F32), 0.0)
    w = lax.all_gather(swapped, "req", axis=0, tiled=True)
    entry, w = lax.optimization_barrier((feedforward_entry_proj, w))
    key_rows = lax.all_gather(entry, "req", axis=0, tiled=True)
    exit_proj, w = lax.optimization_barrier((feedforward_exit_proj, w))
    value_rows = lax.all_gather(exit_proj, "req", axis=0, tiled=True)

    terms, state = time_mix(
        partition_arrangement, prompt_extents, x, carried[0:1], gains, prior_step_blends, w,
        gating_projection, forgetting_left_lowrank, forgetting_right_lowrank,
        forgetting_bias_vector[None], instant_emphasis[None], group_normalizer_scale[None],
        s0, mixing_exit_projection,
    )
    attended = lax.psum(terms, "hid").astype(F32)
    middle = (x.astype(F32) + attended).astype(BF16)
    out_terms, gate_rows = channel_mix(
        middle, carried[1:2], gains, prior_step_blends, feedforward_accept_proj, key_rows, value_rows
    )
    summed = lax.psum_scatter(out_terms, "hid", scatter_dimension=1, tiled=True).astype(F32)
    mid_share = lax.dynamic_slice_in_dim(middle, lax.axis_index("hid") * lw, lw, 1).astype(F32)
    present = jnp.arange(rows) < length
    combined = mid_share + gate_rows * summed
    layer_out = jnp.where(present[:, None], combined, 0.0).astype(BF16)[None]
    last = length - 1
    shift_out = jnp.stack(
        [
            norm_row(lax.dynamic_index_in_dim(x, last, 0, keepdims=False).astype(F32), gains[0]),
            norm_row(lax.dynamic_index_in_dim(middle, last, 0, keepdims=False).astype(F32), gains[1]),
        ]
    ).astype(BF16)[None]
    return (layer_out, state[None], shift_out)


def solution(mesh):
    placed = (
        P("req", None, None),
        P("req"),
        P("req"),
        P("req"),
        P(),
        P(("req", "hid"), None),
        P(("req", "hid"), None),
        P(("req", "hid"), None),
        P(),
        P(),
        P("hid"),
        P(),
        P(None, "hid"),
        P("hid"),
        P("hid"),
        P(None, "hid"),
        P("hid", None),
        P("req", "hid", None, None, None),
        P("req", None, None),
        P(("req", "hid"), None),
        P(("req", "hid"), None),
        P(None, "hid"),
    )
    return jax.shard_map(
        local,
        mesh=mesh,
        in_specs=placed,
        out_specs=(P("req", None, "hid"), P("req", "hid", None, None), P("req", None, None)),
        check_vma=False,
    )
```

```python
from functools import partial

import jax
import jax.numpy as jnp
from jax import lax
from jax.experimental import pallas as pl
from jax.experimental.pallas import tpu as pltpu
from jax.sharding import PartitionSpec as P

HEAD = 64
CHUNK = 16
TILE = 64
PAIR = 128
KC = 512
VMEM_LIMIT = 58 * 1024 * 1024
F32 = jnp.float32
BF16 = jnp.bfloat16
MESH = pl.DeviceIdType.MESH
NY, NZ, NC = 2, 4, 2
NX, NW = 4, 2
PIECES = NX * NW
COST = pl.CostEstimate(flops=40_000_000_000, bytes_accessed=40_000_000, transcendentals=0)
VM = pl.BlockSpec(memory_space=pltpu.VMEM)
SM = pl.BlockSpec(memory_space=pltpu.SMEM)
HB = pl.BlockSpec(memory_space=pl.ANY)


def nt_dot(a, b):
    return lax.dot_general(a, b, (((1,), (1,)), ((), ())), preferred_element_type=F32)


def tn_dot(a, b):
    return lax.dot_general(a, b, (((0,), (0,)), ((), ())), preferred_element_type=F32)


def nn_dot(a, b):
    return jnp.dot(a, b, preferred_element_type=F32)


def piece_owners():
    x, w = lax.axis_index("req") // NW, lax.axis_index("req") % NW

    def at(dx, other):
        return (x + dx) % NX * NW + (1 - w if other else w)

    return [at(0, 0), at(0, 1), at(NX - 1, 0), at(1, 0), at(NX - 1, 1), at(1, 1), at(2, 0), at(2, 1)]


def collect(own):
    def send(value, dx, dw):
        pairs = [
            (x * NW + w, (x + dx) % NX * NW + (w + dw) % NW) for x in range(NX) for w in range(NW)
        ]
        return lax.ppermute(value, "req", pairs)

    other = send(own, 0, 1)
    before, after = send(own, 1, 0), send(own, NX - 1, 0)
    before_other, after_other = send(other, 1, 0), send(other, NX - 1, 0)
    far, far_other = send(before, 1, 0), send(after_other, NX - 1, 0)
    return [own, other, before, after, before_other, after_other, far, far_other]


def group_columns(g, lw):
    block = (g % NY) * (NZ * NC) + (g // NY % NZ) * NC + g // (NY * NZ)
    return pl.ds(pl.multiple_of(block * lw, lw), lw)


def row_stats(part, count, rows, width, eps):
    def add_sum(c, total):
        return total + jnp.sum(part(c), axis=1, keepdims=True)

    def add_square(c, total):
        center = part(c) - mean
        return total + jnp.sum(center * center, axis=1, keepdims=True)

    zero = jnp.zeros((rows, 1), F32)
    mean = lax.fori_loop(0, count, add_sum, zero) / width
    var = lax.fori_loop(0, count, add_square, zero) / width
    return mean, 1.0 / jnp.sqrt(var + eps)


def normed_and_delta(part, first_ref, gain_ref, which, cols, mean, inv):
    normed = (part - mean) * inv * gain_ref[:, cols].astype(F32)[which : which + 1]
    before = pltpu.roll(normed, 1, 0)
    row = lax.broadcasted_iota(jnp.int32, normed.shape, 0)
    before = jnp.where(row == 0, first_ref[:, cols], before)
    return normed, before - normed


def pick_row(values, index):
    row = lax.broadcasted_iota(jnp.int32, values.shape, 0)
    return jnp.sum(jnp.where(row == index, values, 0.0), axis=0, keepdims=True)


def time_mix_kernel(
    perm_ref, len_ref, x_ref, first_ref, gain_ref, mix_ref, gating_ref, left_ref,
    right_ref, bias_ref, bonus_ref, gscale_ref, s0_ref, exit_ref, *refs,
):
    pieces = refs[:PIECES]
    terms_ref, state_ref, last_ref = refs[PIECES : PIECES + 3]
    (
        w_scr, acc, acc_low, acc_gate, logw_scr, prod_scr, gated_scr, st_scr, sem,
    ) = refs[PIECES + 3 :]
    rows, width = x_ref.shape
    block_rows = w_scr.shape[1]
    lw = acc_gate.shape[1]

    for piece, owner in zip(pieces, piece_owners()):
        count = piece.shape[0]

        def start(j, carry, piece=piece, base=owner * count):
            pltpu.make_async_copy(piece.at[j], w_scr.at[perm_ref[base + j]], sem).start()
            return carry

        lax.fori_loop(0, count, start, 0)

    def part(c):
        return x_ref[:, pl.ds(pl.multiple_of(c * KC, KC), KC)].astype(F32)

    mean, inv = row_stats(part, width // KC, rows, width, 1e-05)
    acc[...] = jnp.zeros_like(acc)
    acc_low[...] = jnp.zeros_like(acc_low)
    acc_gate[...] = jnp.zeros_like(acc_gate)
    pltpu.make_async_copy(w_scr, w_scr, sem).wait()
    per = KC // block_rows

    def project(c, carry):
        cols = pl.ds(pl.multiple_of(c * KC, KC), KC)
        normed, delta = normed_and_delta(part(c), first_ref, gain_ref, 0, cols, mean, inv)
        last_ref[:, cols] = pick_row(normed, len_ref[0] - 1)
        mix = mix_ref[:, cols].astype(F32)

        def blend(m):
            return (normed + delta * mix[m : m + 1]).astype(BF16)

        for m in range(3):
            wm = w_scr[pl.ds(c * per, per), :, m * lw : (m + 1) * lw].reshape(KC, lw)
            acc[:, m * lw : (m + 1) * lw] += nn_dot(blend(m), wm)
        acc_low[...] += nn_dot(blend(3), left_ref[cols, :])
        acc_gate[...] += nn_dot(blend(4), gating_ref[cols, :])
        return carry

    lax.fori_loop(0, width // KC, project, 0)
    length = len_ref[0]
    present = lax.broadcasted_iota(jnp.int32, (rows, lw), 0) < length
    low = jnp.tanh(acc_low[...]).astype(BF16)
    log_decay = -jnp.exp(bias_ref[...] + nn_dot(low, right_ref[...]))
    logw_scr[...] = jnp.where(present, log_decay, 0.0)
    acc[:, lw : 2 * lw] = jnp.where(present, acc[:, lw : 2 * lw], 0.0)

    pairs = lw // PAIR
    hole = jnp.zeros((HEAD, HEAD), F32)
    for p in range(pairs):
        top = jnp.concatenate([s0_ref[2 * p], hole], axis=1)
        bottom = jnp.concatenate([hole, s0_ref[2 * p + 1]], axis=1)
        st_scr[p] = jnp.concatenate([top, bottom], axis=0).T

    def same_head(size):
        a = lax.broadcasted_iota(jnp.int32, (size, size), 0) // HEAD
        b = lax.broadcasted_iota(jnp.int32, (size, size), 1) // HEAD
        return a == b

    ones = jnp.where(same_head(lw), 1.0, 0.0).astype(BF16)
    pair_mask = same_head(PAIR)
    slot = lax.broadcasted_iota(jnp.int32, (TILE, lw), 0) % CHUNK

    def head_sum(values):
        high = values.astype(BF16)
        rest = (values - high.astype(F32)).astype(BF16)
        return nn_dot(high, ones) + nn_dot(rest, ones)

    def tile_step(t, carry):
        here = pl.ds(pl.multiple_of(t * TILE, TILE), TILE)
        r = acc[here, 0:lw]
        k = acc[here, lw : 2 * lw]
        v = acc[here, 2 * lw : 3 * lw]
        decay = logw_scr[here, :]
        incl = decay
        step = 1
        while step < CHUNK:
            incl = incl + jnp.where(slot >= step, pltpu.roll(incl, step, 0), 0.0)
            step *= 2
        excl = incl - decay
        prod_scr[0:TILE, :] = (r * bonus_ref[...] * k).astype(BF16)
        for d in range(1, CHUNK):
            gap = jnp.minimum(excl - pltpu.roll(incl, d, 0), 0.0)
            term = jnp.where(slot >= d, r * pltpu.roll(k, d, 0) * jnp.exp(gap), 0.0)
            prod_scr[d * TILE : (d + 1) * TILE, :] = term.astype(BF16)
        scores = nn_dot(prod_scr[...], ones)
        out = scores[0:TILE] * v
        for d in range(1, CHUNK):
            out = out + scores[d * TILE : (d + 1) * TILE] * pltpu.roll(v, d, 0)
        rw = (r * jnp.exp(excl)).astype(BF16)
        vb = v.astype(BF16)
        pieces = []
        for c in range(TILE // CHUNK):
            lo, hi = c * CHUNK, (c + 1) * CHUNK
            closing = incl[hi - 1 : hi]
            kw = (k[lo:hi] * jnp.exp(closing - incl[lo:hi])).astype(BF16)
            fade = jnp.exp(closing)
            parts = []
            for p in range(pairs):
                a, b = p * PAIR, (p + 1) * PAIR
                st = st_scr[p]
                parts.append(nt_dot(rw[lo:hi, a:b], st.astype(BF16)))
                grown = tn_dot(vb[lo:hi, a:b], kw[:, a:b])
                st_scr[p] = st * fade[:, a:b] + jnp.where(pair_mask, grown, 0.0)
            pieces.append(jnp.concatenate(parts, axis=1))
        out = out + jnp.concatenate(pieces, axis=0)
        center = out - head_sum(out) * (1.0 / HEAD)
        spread = head_sum(center * center) * (1.0 / HEAD)
        grouped = center / jnp.sqrt(spread + 0.00064) * gscale_ref[...]
        g = acc_gate[here, :]
        gate = g / (1.0 + jnp.exp(-g))
        gated_scr[here, :] = (grouped * gate).astype(BF16)
        return carry

    lax.fori_loop(0, rows // TILE, tile_step, 0)
    for p in range(pairs):
        full = st_scr[p].T
        state_ref[2 * p] = full[0:HEAD, 0:HEAD]
        state_ref[2 * p + 1] = full[HEAD:PAIR, HEAD:PAIR]

    def leave(g, carry):
        terms_ref[g] = nn_dot(gated_scr[...], exit_ref[:, group_columns(g, lw)]).astype(BF16)
        return carry

    lax.fori_loop(0, width // lw, leave, 0)


def time_mix(perm, length, x, first, gains, mixes, gating, left, right, bias, bonus, gscale, s0, exit_w, pieces):
    rows, width = x.shape
    lw = gating.shape[1]
    piece_blocks, block_rows, piece_width = pieces[0].shape
    return pl.pallas_call(
        time_mix_kernel,
        out_shape=(
            jax.ShapeDtypeStruct((width // lw, rows, lw), BF16),
            jax.ShapeDtypeStruct(s0.shape, F32),
            jax.ShapeDtypeStruct((1, width), F32),
        ),
        in_specs=[SM, SM] + [VM] * 12 + [HB] * PIECES,
        out_specs=(VM, VM, VM),
        scratch_shapes=[
            pltpu.VMEM((PIECES * piece_blocks, block_rows, piece_width), BF16),
            pltpu.VMEM((rows, 3 * lw), F32),
            pltpu.VMEM((rows, left.shape[1]), F32),
            pltpu.VMEM((rows, lw), F32),
            pltpu.VMEM((rows, lw), F32),
            pltpu.VMEM((CHUNK * TILE, lw), BF16),
            pltpu.VMEM((rows, lw), BF16),
            pltpu.VMEM((lw // PAIR, PAIR, PAIR), F32),
            pltpu.SemaphoreType.DMA,
        ],
        compiler_params=pltpu.CompilerParams(vmem_limit_bytes=VMEM_LIMIT),
        cost_estimate=COST,
        name="time_mix",
    )(perm, length, x, first, gains, mixes, gating, left, right, bias, bonus, gscale, s0, exit_w, *pieces)


def channel_mix_kernel(
    len_ref, x_ref, first_ref, gain_ref, mix_ref, accept_ref, *refs,
):
    keys, values = refs[:PIECES], refs[PIECES : 2 * PIECES]
    terms_ref, gate_ref, last_ref = refs[2 * PIECES : 2 * PIECES + 3]
    key_scr, value_scr, inner, acc_gate, hidden, key_sems, value_sems = refs[2 * PIECES + 3 :]
    groups, rows, lw = x_ref.shape
    units = keys[0].shape[0]

    def fetch(pieces, scr, sems):
        copies = [
            pltpu.make_async_copy(piece, scr.at[pl.ds(i * units, units)], sems.at[i])
            for i, piece in enumerate(pieces)
        ]
        for copy in copies:
            copy.start()
        return copies

    key_copies = fetch(keys, key_scr, key_sems)
    value_copies = fetch(values, value_scr, value_sems)

    def part(g):
        return x_ref[g].astype(F32)

    mean, inv = row_stats(part, groups, rows, groups * lw, 1e-05)
    inner[...] = jnp.zeros_like(inner)
    acc_gate[...] = jnp.zeros_like(acc_gate)
    for copy in key_copies:
        copy.wait()

    def project(g, carry):
        cols = group_columns(g, lw)
        normed, delta = normed_and_delta(part(g), first_ref, gain_ref, 1, cols, mean, inv)
        last_ref[:, cols] = pick_row(normed, len_ref[0] - 1)
        mix = mix_ref[:, cols].astype(F32)
        inner[...] += nt_dot((normed + delta * mix[5:6]).astype(BF16), key_scr[:, cols])
        acc_gate[...] += nn_dot((normed + delta * mix[6:7]).astype(BF16), accept_ref[cols, :])
        return carry

    lax.fori_loop(0, groups, project, 0)
    positive = jnp.maximum(inner[...], 0.0)
    hidden[...] = (positive * positive).astype(BF16)
    gate_ref[...] = jax.nn.sigmoid(acc_gate[...])
    for copy in value_copies:
        copy.wait()

    def leave(g, carry):
        terms_ref[g] = nn_dot(hidden[...], value_scr[:, group_columns(g, lw)]).astype(BF16)
        return carry

    lax.fori_loop(0, groups, leave, 0)


def channel_mix(length, x, first, gains, mixes, accept, keys, values):
    groups, rows, lw = x.shape
    units = PIECES * keys[0].shape[0]
    width = groups * lw
    return pl.pallas_call(
        channel_mix_kernel,
        out_shape=(
            jax.ShapeDtypeStruct((groups, rows, lw), BF16),
            jax.ShapeDtypeStruct((rows, lw), F32),
            jax.ShapeDtypeStruct((1, groups * lw), F32),
        ),
        in_specs=[SM] + [VM] * 5 + [HB] * (2 * PIECES),
        out_specs=(VM, VM, VM),
        scratch_shapes=[
            pltpu.VMEM((units, width), BF16),
            pltpu.VMEM((units, width), BF16),
            pltpu.VMEM((rows, units), F32),
            pltpu.VMEM((rows, lw), F32),
            pltpu.VMEM((rows, units), BF16),
            pltpu.SemaphoreType.DMA((PIECES,)),
            pltpu.SemaphoreType.DMA((PIECES,)),
        ],
        compiler_params=pltpu.CompilerParams(vmem_limit_bytes=VMEM_LIMIT),
        cost_estimate=COST,
        name="channel_mix",
    )(length, x, first, gains, mixes, accept, *keys, *values)


def hid_place():
    me = lax.axis_index("hid")
    y, z, c = me // (NZ * NC), me // NC % NZ, me % NC

    def at(yy, zz, cc):
        return {"hid": (yy * NZ + zz) * NC + cc}

    zu, zd = (z + 1) % NZ, (z + 3) % NZ
    peers = {"core": at(y, z, 1 - c), "up": at(y, zu, c), "down": at(y, zd, c), "y": at(1 - y, z, c)}
    return y, z, c, zu, (z + 2) % NZ, zd, peers


def meet(peers):
    barrier = pltpu.get_barrier_semaphore()
    for device in peers.values():
        pl.semaphore_signal(barrier, inc=1, device_id=device, device_id_type=MESH)
    pl.semaphore_wait(barrier, len(peers))


class Copies:
    def __init__(self, send, recv):
        self.send, self.recv, self.made = send, recv, []

    def start(self, src, dst, device):
        i = len(self.made)
        copy = pltpu.make_async_remote_copy(
            src_ref=src, dst_ref=dst, send_sem=self.send.at[i], recv_sem=self.recv.at[i],
            device_id=device, device_id_type=MESH,
        )
        copy.start()
        self.made.append(copy)
        return copy

    def finish(self):
        for copy in self.made:
            copy.wait_send()


def sum_terms(terms, acc, core_buf, pass_buf, near_buf, y_buf, copies, place):
    y, z, c, zu, z2, zd, peers = place
    half = terms.shape[3] // 2
    from_core = [
        copies.start(terms.at[1 - c, g], core_buf.at[g], peers["core"]) for g in (z2, zu, zd, z)
    ]

    def add_core(i, g):
        from_core[i].wait_recv()
        acc[g] = (terms[c, g].astype(F32) + core_buf[g].astype(F32)).astype(BF16)

    add_core(0, z2)
    first_up = copies.start(acc.at[z2, :, 0:half], pass_buf.at[0], peers["up"])
    first_down = copies.start(acc.at[z2, :, half : 2 * half], pass_buf.at[1], peers["down"])
    add_core(1, zu)
    add_core(2, zd)
    first_up.wait_recv()
    acc[zu, :, 0:half] = (acc[zu, :, 0:half].astype(F32) + pass_buf[0].astype(F32)).astype(BF16)
    second_up = copies.start(acc.at[zu], near_buf.at[0], peers["up"])
    first_down.wait_recv()
    acc[zd, :, half : 2 * half] = (
        acc[zd, :, half : 2 * half].astype(F32) + pass_buf[1].astype(F32)
    ).astype(BF16)
    second_down = copies.start(acc.at[zd], near_buf.at[1], peers["down"])
    add_core(3, z)
    second_up.wait_recv()
    second_down.wait_recv()

    def total_of(yy):
        return acc[z, yy].astype(F32) + near_buf[0, yy].astype(F32) + near_buf[1, yy].astype(F32)

    acc[z, 1 - y] = total_of(1 - y).astype(BF16)
    across = copies.start(acc.at[z, 1 - y], y_buf, peers["y"])
    own = total_of(y)
    across.wait_recv()
    return own + y_buf[...].astype(F32)


def sum_scratch(shape, copies):
    nc, nz, ny, rows, lw = shape
    return [
        pltpu.VMEM((nz, ny, rows, lw), BF16),
        pltpu.VMEM((nz, ny, rows, lw), BF16),
        pltpu.VMEM((2, ny, rows // 2, lw), BF16),
        pltpu.VMEM((2, ny, rows, lw), BF16),
        pltpu.VMEM((rows, lw), BF16),
        pltpu.SemaphoreType.DMA((copies,)),
        pltpu.SemaphoreType.DMA((copies,)),
    ]


def join_kernel(terms, x_ref, mid_ref, own_ref, acc, core_buf, pass_buf, near_buf, y_buf, send, recv):
    place = hid_place()
    y, z, c, zu, z2, zd, peers = place
    meet(peers)
    copies = Copies(send, recv)
    half = x_ref.shape[0] // 2
    total = sum_terms(terms, acc, core_buf, pass_buf, near_buf, y_buf, copies, place)
    own = (x_ref[...].astype(F32) + total).astype(BF16)
    own_ref[...] = own
    mid_ref[c, z, y] = own

    def pass_on(index, device):
        return copies.start(mid_ref.at[index], mid_ref.at[index], device)

    pass_on((c, z, y), peers["y"]).wait_recv()
    up = pass_on((c, z), peers["up"])
    down = pass_on((c, z), peers["down"])
    waits = [pass_on((c, z), peers["core"])]
    up.wait_recv()
    far = [pass_on((c, zd, slice(None), slice(0, half)), peers["up"])]
    waits.append(pass_on((c, zd), peers["core"]))
    down.wait_recv()
    far.append(pass_on((c, zu, slice(None), slice(half, 2 * half)), peers["down"]))
    waits.append(pass_on((c, zu), peers["core"]))
    for copy in far:
        copy.wait_recv()
    waits.append(pass_on((c, z2), peers["core"]))
    for copy in waits:
        copy.wait_recv()
    copies.finish()


def join(terms, x_share):
    rows, lw = x_share.shape
    shape = (NC, NZ, NY, rows, lw)
    return pl.pallas_call(
        join_kernel,
        out_shape=(jax.ShapeDtypeStruct(shape, BF16), jax.ShapeDtypeStruct((rows, lw), BF16)),
        in_specs=[VM, VM],
        out_specs=(VM, VM),
        scratch_shapes=sum_scratch(shape, 18),
        compiler_params=pltpu.CompilerParams(
            collective_id=0, has_side_effects=True, vmem_limit_bytes=VMEM_LIMIT
        ),
        cost_estimate=COST,
        name="join",
    )(terms.reshape(shape), x_share)


def close_kernel(
    len_ref, terms, own_ref, gate_ref, out_ref, acc, core_buf, pass_buf, near_buf, y_buf, send, recv
):
    place = hid_place()
    meet(place[-1])
    copies = Copies(send, recv)
    total = sum_terms(terms, acc, core_buf, pass_buf, near_buf, y_buf, copies, place)
    combined = own_ref[...].astype(F32) + gate_ref[...] * total
    row = lax.broadcasted_iota(jnp.int32, combined.shape, 0)
    out_ref[...] = jnp.where(row < len_ref[0], combined, 0.0).astype(BF16)
    copies.finish()


def close(length, terms, own, gate_rows):
    rows, lw = own.shape
    shape = (NC, NZ, NY, rows, lw)
    return pl.pallas_call(
        close_kernel,
        out_shape=jax.ShapeDtypeStruct((rows, lw), BF16),
        in_specs=[SM, VM, VM, VM],
        out_specs=VM,
        scratch_shapes=sum_scratch(shape, 9),
        compiler_params=pltpu.CompilerParams(
            collective_id=1, has_side_effects=True, vmem_limit_bytes=VMEM_LIMIT
        ),
        name="close",
    )(length, terms.reshape(shape), own, gate_rows)


def local(
    input_activations,
    prompt_extents,
    continuing_flags,
    owning_index,
    partition_arrangement,
    training_accept_pieces,
    training_lookup_pieces,
    training_content_pieces,
    normalizer_scales,
    prior_step_blends,
    forgetting_bias_vector,
    forgetting_left_lowrank,
    forgetting_right_lowrank,
    instant_emphasis,
    group_normalizer_scale,
    gating_projection,
    mixing_exit_projection,
    kept_summary_places,
    previous_normed_entries,
    feedforward_entry_proj,
    feedforward_exit_proj,
    feedforward_accept_proj,
):
    x = input_activations[0]
    rows, width = x.shape
    lw = mixing_exit_projection.shape[0]
    hid = lax.axis_size("hid")
    block_rows = training_accept_pieces.shape[0]
    resuming = continuing_flags[0]
    gains = normalizer_scales.astype(F32)
    carried = jnp.where(resuming == 1, previous_normed_entries[0].astype(F32), 0.0)

    own = jnp.stack([training_accept_pieces, training_lookup_pieces, training_content_pieces])
    own = own.astype(BF16).reshape(3, block_rows, hid, lw).transpose(2, 1, 0, 3)
    own = own.reshape(hid, block_rows, 3 * lw)
    swapped = lax.all_to_all(own, "hid", split_axis=0, concat_axis=0, tiled=True)
    fetched = lax.all_to_all(
        kept_summary_places[0, 0].astype(BF16).reshape(hid, -1, HEAD, HEAD),
        "hid", split_axis=0, concat_axis=0, tiled=True,
    )
    chosen = lax.dynamic_index_in_dim(fetched, owning_index[0], 0, keepdims=False)
    s0 = jnp.where(resuming == 1, chosen.astype(F32), 0.0)
    pieces = collect(swapped)
    entry, exit_proj, pieces[4], pieces[5] = lax.optimization_barrier(
        (feedforward_entry_proj, feedforward_exit_proj, pieces[4], pieces[5])
    )
    keys = collect(entry)
    values = collect(exit_proj)

    terms, state, last_in = time_mix(
        partition_arrangement, prompt_extents, x, carried[0:1], gains, prior_step_blends,
        gating_projection, forgetting_left_lowrank, forgetting_right_lowrank,
        forgetting_bias_vector[None], instant_emphasis[None], group_normalizer_scale[None],
        s0, mixing_exit_projection, pieces,
    )
    x_share = lax.dynamic_slice_in_dim(x, lax.axis_index("hid") * lw, lw, 1)
    middle, own_middle = join(terms, x_share)
    out_terms, gate_rows, last_chan = channel_mix(
        prompt_extents, middle.reshape(hid, rows, lw), carried[1:2], gains, prior_step_blends,
        feedforward_accept_proj, keys, values,
    )
    layer_out = close(prompt_extents, out_terms, own_middle, gate_rows)[None]
    shift_out = jnp.concatenate([last_in, last_chan]).astype(BF16)[None]
    return (layer_out, state[None], shift_out)


def solution(mesh):
    placed = (
        P("req", None, None),
        P("req"),
        P("req"),
        P("req"),
        P(),
        P(("req", "hid"), None),
        P(("req", "hid"), None),
        P(("req", "hid"), None),
        P(),
        P(),
        P("hid"),
        P(),
        P(None, "hid"),
        P("hid"),
        P("hid"),
        P(None, "hid"),
        P("hid", None),
        P("req", "hid", None, None, None),
        P("req", None, None),
        P(("req", "hid"), None),
        P(("req", "hid"), None),
        P(None, "hid"),
    )
    return jax.shard_map(
        local,
        mesh=mesh,
        in_specs=placed,
        out_specs=(P("req", None, "hid"), P("req", "hid", None, None), P("req", None, None)),
        check_vma=False,
    )
```

```python
from functools import partial

import jax
import jax.numpy as jnp
from jax import lax
from jax.experimental import pallas as pl
from jax.experimental.pallas import tpu as pltpu
from jax.sharding import PartitionSpec as P

HEAD = 64
CHUNK = 16
TILE = 64
PAIR = 128
KC = 512
VMEM_LIMIT = 58 * 1024 * 1024
F32 = jnp.float32
BF16 = jnp.bfloat16
MESH = pl.DeviceIdType.MESH
NY, NZ, NC = 2, 4, 2
NX, NW = 4, 2
PIECES = NX * NW
COST = pl.CostEstimate(flops=40_000_000_000, bytes_accessed=40_000_000, transcendentals=0)
VM = pl.BlockSpec(memory_space=pltpu.VMEM)
SM = pl.BlockSpec(memory_space=pltpu.SMEM)
HB = pl.BlockSpec(memory_space=pl.ANY)


def nt_dot(a, b):
    return lax.dot_general(a, b, (((1,), (1,)), ((), ())), preferred_element_type=F32)


def tn_dot(a, b):
    return lax.dot_general(a, b, (((0,), (0,)), ((), ())), preferred_element_type=F32)


def nn_dot(a, b):
    return jnp.dot(a, b, preferred_element_type=F32)


def piece_owners():
    x, w = lax.axis_index("req") // NW, lax.axis_index("req") % NW

    def at(dx, other):
        return (x + dx) % NX * NW + (1 - w if other else w)

    return [at(0, 0), at(0, 1), at(NX - 1, 0), at(1, 0), at(NX - 1, 1), at(1, 1), at(2, 0), at(2, 1)]


def send(value, dx, dw):
    pairs = [(x * NW + w, (x + dx) % NX * NW + (w + dw) % NW) for x in range(NX) for w in range(NW)]
    return lax.ppermute(value, "req", pairs)


def first_hop(own):
    return [own, send(own, 0, 1), send(own, 1, 0), send(own, NX - 1, 0)]


def second_hop(have):
    other = have[1]
    return have + [send(other, 1, 0), send(other, NX - 1, 0)]


def third_hop(have):
    return have + [send(have[2], 1, 0), send(have[5], NX - 1, 0)]


def group_columns(g, lw):
    block = (g % NY) * (NZ * NC) + (g // NY % NZ) * NC + g // (NY * NZ)
    return pl.ds(pl.multiple_of(block * lw, lw), lw)


def row_stats(part, count, rows, width, eps):
    def add_sum(c, total):
        return total + jnp.sum(part(c), axis=1, keepdims=True)

    def add_square(c, total):
        center = part(c) - mean
        return total + jnp.sum(center * center, axis=1, keepdims=True)

    zero = jnp.zeros((rows, 1), F32)
    mean = lax.fori_loop(0, count, add_sum, zero) / width
    var = lax.fori_loop(0, count, add_square, zero) / width
    return mean, 1.0 / jnp.sqrt(var + eps)


def normed_and_delta(part, first_ref, gain_ref, which, cols, mean, inv):
    normed = (part - mean) * inv * gain_ref[:, cols].astype(F32)[which : which + 1]
    before = pltpu.roll(normed, 1, 0)
    row = lax.broadcasted_iota(jnp.int32, normed.shape, 0)
    before = jnp.where(row == 0, first_ref[:, cols], before)
    return normed, before - normed


def pick_row(values, index):
    row = lax.broadcasted_iota(jnp.int32, values.shape, 0)
    return jnp.sum(jnp.where(row == index, values, 0.0), axis=0, keepdims=True)


def time_mix_kernel(
    perm_ref, len_ref, x_ref, first_ref, gain_ref, mix_ref, gating_ref, left_ref,
    right_ref, bias_ref, bonus_ref, gscale_ref, s0_ref, exit_ref, *refs,
):
    pieces = refs[:PIECES]
    terms_ref, state_ref, last_ref = refs[PIECES : PIECES + 3]
    (
        w_scr, acc, acc_low, acc_gate, logw_scr, prod_scr, gated_scr, st_scr, sem,
    ) = refs[PIECES + 3 :]
    rows, width = x_ref.shape
    block_rows = w_scr.shape[1]
    lw = acc_gate.shape[1]

    for piece, owner in zip(pieces, piece_owners()):
        count = piece.shape[0]

        def start(j, carry, piece=piece, base=owner * count):
            pltpu.make_async_copy(piece.at[j], w_scr.at[perm_ref[base + j]], sem).start()
            return carry

        lax.fori_loop(0, count, start, 0)

    def part(c):
        return x_ref[:, pl.ds(pl.multiple_of(c * KC, KC), KC)].astype(F32)

    mean, inv = row_stats(part, width // KC, rows, width, 1e-05)
    acc[...] = jnp.zeros_like(acc)
    acc_low[...] = jnp.zeros_like(acc_low)
    acc_gate[...] = jnp.zeros_like(acc_gate)
    pltpu.make_async_copy(w_scr, w_scr, sem).wait()
    per = KC // block_rows

    def project(c, carry):
        cols = pl.ds(pl.multiple_of(c * KC, KC), KC)
        normed, delta = normed_and_delta(part(c), first_ref, gain_ref, 0, cols, mean, inv)
        last_ref[:, cols] = pick_row(normed, len_ref[0] - 1)
        mix = mix_ref[:, cols].astype(F32)

        def blend(m):
            return (normed + delta * mix[m : m + 1]).astype(BF16)

        for m in range(3):
            wm = w_scr[pl.ds(c * per, per), :, m * lw : (m + 1) * lw].reshape(KC, lw)
            acc[:, m * lw : (m + 1) * lw] += nn_dot(blend(m), wm)
        acc_low[...] += nn_dot(blend(3), left_ref[cols, :])
        acc_gate[...] += nn_dot(blend(4), gating_ref[cols, :])
        return carry

    lax.fori_loop(0, width // KC, project, 0)
    length = len_ref[0]
    present = lax.broadcasted_iota(jnp.int32, (rows, lw), 0) < length
    low = jnp.tanh(acc_low[...]).astype(BF16)
    log_decay = -jnp.exp(bias_ref[...] + nn_dot(low, right_ref[...]))
    logw_scr[...] = jnp.where(present, log_decay, 0.0)
    acc[:, lw : 2 * lw] = jnp.where(present, acc[:, lw : 2 * lw], 0.0)

    pairs = lw // PAIR
    hole = jnp.zeros((HEAD, HEAD), F32)
    for p in range(pairs):
        top = jnp.concatenate([s0_ref[2 * p], hole], axis=1)
        bottom = jnp.concatenate([hole, s0_ref[2 * p + 1]], axis=1)
        st_scr[p] = jnp.concatenate([top, bottom], axis=0).T

    def same_head(size):
        a = lax.broadcasted_iota(jnp.int32, (size, size), 0) // HEAD
        b = lax.broadcasted_iota(jnp.int32, (size, size), 1) // HEAD
        return a == b

    ones = jnp.where(same_head(lw), 1.0, 0.0).astype(BF16)
    pair_mask = same_head(PAIR)
    slot = lax.broadcasted_iota(jnp.int32, (TILE, lw), 0) % CHUNK

    def head_sum(values):
        high = values.astype(BF16)
        rest = (values - high.astype(F32)).astype(BF16)
        return nn_dot(high, ones) + nn_dot(rest, ones)

    def tile_step(t, carry):
        here = pl.ds(pl.multiple_of(t * TILE, TILE), TILE)
        r = acc[here, 0:lw]
        k = acc[here, lw : 2 * lw]
        v = acc[here, 2 * lw : 3 * lw]
        decay = logw_scr[here, :]
        incl = decay
        step = 1
        while step < CHUNK:
            incl = incl + jnp.where(slot >= step, pltpu.roll(incl, step, 0), 0.0)
            step *= 2
        excl = incl - decay
        prod_scr[0:TILE, :] = (r * bonus_ref[...] * k).astype(BF16)
        for d in range(1, CHUNK):
            gap = jnp.minimum(excl - pltpu.roll(incl, d, 0), 0.0)
            term = jnp.where(slot >= d, r * pltpu.roll(k, d, 0) * jnp.exp(gap), 0.0)
            prod_scr[d * TILE : (d + 1) * TILE, :] = term.astype(BF16)
        scores = nn_dot(prod_scr[...], ones)
        out = scores[0:TILE] * v
        for d in range(1, CHUNK):
            out = out + scores[d * TILE : (d + 1) * TILE] * pltpu.roll(v, d, 0)
        rw = (r * jnp.exp(excl)).astype(BF16)
        vb = v.astype(BF16)
        pieces = []
        for c in range(TILE // CHUNK):
            lo, hi = c * CHUNK, (c + 1) * CHUNK
            closing = incl[hi - 1 : hi]
            kw = (k[lo:hi] * jnp.exp(closing - incl[lo:hi])).astype(BF16)
            fade = jnp.exp(closing)
            parts = []
            for p in range(pairs):
                a, b = p * PAIR, (p + 1) * PAIR
                st = st_scr[p]
                parts.append(nt_dot(rw[lo:hi, a:b], st.astype(BF16)))
                grown = tn_dot(vb[lo:hi, a:b], kw[:, a:b])
                st_scr[p] = st * fade[:, a:b] + jnp.where(pair_mask, grown, 0.0)
            pieces.append(jnp.concatenate(parts, axis=1))
        out = out + jnp.concatenate(pieces, axis=0)
        center = out - head_sum(out) * (1.0 / HEAD)
        spread = head_sum(center * center) * (1.0 / HEAD)
        grouped = center / jnp.sqrt(spread + 0.00064) * gscale_ref[...]
        g = acc_gate[here, :]
        gate = g / (1.0 + jnp.exp(-g))
        gated_scr[here, :] = (grouped * gate).astype(BF16)
        return carry

    lax.fori_loop(0, rows // TILE, tile_step, 0)
    for p in range(pairs):
        full = st_scr[p].T
        state_ref[2 * p] = full[0:HEAD, 0:HEAD]
        state_ref[2 * p + 1] = full[HEAD:PAIR, HEAD:PAIR]

    def leave(g, carry):
        terms_ref[g] = nn_dot(gated_scr[...], exit_ref[:, group_columns(g, lw)]).astype(BF16)
        return carry

    lax.fori_loop(0, width // lw, leave, 0)


def time_mix(perm, length, x, first, gains, mixes, gating, left, right, bias, bonus, gscale, s0, exit_w, pieces):
    rows, width = x.shape
    lw = gating.shape[1]
    piece_blocks, block_rows, piece_width = pieces[0].shape
    return pl.pallas_call(
        time_mix_kernel,
        out_shape=(
            jax.ShapeDtypeStruct((width // lw, rows, lw), BF16),
            jax.ShapeDtypeStruct(s0.shape, F32),
            jax.ShapeDtypeStruct((1, width), F32),
        ),
        in_specs=[SM, SM] + [VM] * 12 + [HB] * PIECES,
        out_specs=(VM, VM, VM),
        scratch_shapes=[
            pltpu.VMEM((PIECES * piece_blocks, block_rows, piece_width), BF16),
            pltpu.VMEM((rows, 3 * lw), F32),
            pltpu.VMEM((rows, left.shape[1]), F32),
            pltpu.VMEM((rows, lw), F32),
            pltpu.VMEM((rows, lw), F32),
            pltpu.VMEM((CHUNK * TILE, lw), BF16),
            pltpu.VMEM((rows, lw), BF16),
            pltpu.VMEM((lw // PAIR, PAIR, PAIR), F32),
            pltpu.SemaphoreType.DMA,
        ],
        compiler_params=pltpu.CompilerParams(vmem_limit_bytes=VMEM_LIMIT),
        cost_estimate=COST,
        name="time_mix",
    )(perm, length, x, first, gains, mixes, gating, left, right, bias, bonus, gscale, s0, exit_w, *pieces)


def channel_mix_kernel(
    len_ref, x_ref, first_ref, gain_ref, mix_ref, accept_ref, *refs,
):
    pieces = refs[:PIECES]
    terms_ref, gate_ref, last_ref = refs[PIECES : PIECES + 3]
    key_scr, value_scr, inner, acc_gate, hidden, key_sems, value_sems = refs[PIECES + 3 :]
    groups, rows, lw = x_ref.shape
    units = pieces[0].shape[0] // 2

    def fetch(begin, scr, sems):
        copies = [
            pltpu.make_async_copy(
                piece.at[pl.ds(begin, units)], scr.at[pl.ds(i * units, units)], sems.at[i]
            )
            for i, piece in enumerate(pieces)
        ]
        for copy in copies:
            copy.start()
        return copies

    key_copies = fetch(0, key_scr, key_sems)
    value_copies = fetch(units, value_scr, value_sems)

    def part(g):
        return x_ref[g].astype(F32)

    mean, inv = row_stats(part, groups, rows, groups * lw, 1e-05)
    inner[...] = jnp.zeros_like(inner)
    acc_gate[...] = jnp.zeros_like(acc_gate)
    for copy in key_copies:
        copy.wait()

    def project(g, carry):
        cols = group_columns(g, lw)
        normed, delta = normed_and_delta(part(g), first_ref, gain_ref, 1, cols, mean, inv)
        last_ref[:, cols] = pick_row(normed, len_ref[0] - 1)
        mix = mix_ref[:, cols].astype(F32)
        inner[...] += nt_dot((normed + delta * mix[5:6]).astype(BF16), key_scr[:, cols])
        acc_gate[...] += nn_dot((normed + delta * mix[6:7]).astype(BF16), accept_ref[cols, :])
        return carry

    lax.fori_loop(0, groups, project, 0)
    positive = jnp.maximum(inner[...], 0.0)
    hidden[...] = (positive * positive).astype(BF16)
    gate_ref[...] = jax.nn.sigmoid(acc_gate[...])
    for copy in value_copies:
        copy.wait()

    def leave(g, carry):
        terms_ref[g] = nn_dot(hidden[...], value_scr[:, group_columns(g, lw)]).astype(BF16)
        return carry

    lax.fori_loop(0, groups, leave, 0)


def channel_mix(length, x, first, gains, mixes, accept, pieces):
    groups, rows, lw = x.shape
    units = PIECES * pieces[0].shape[0] // 2
    width = groups * lw
    return pl.pallas_call(
        channel_mix_kernel,
        out_shape=(
            jax.ShapeDtypeStruct((groups, rows, lw), BF16),
            jax.ShapeDtypeStruct((rows, lw), F32),
            jax.ShapeDtypeStruct((1, groups * lw), F32),
        ),
        in_specs=[SM] + [VM] * 5 + [HB] * PIECES,
        out_specs=(VM, VM, VM),
        scratch_shapes=[
            pltpu.VMEM((units, width), BF16),
            pltpu.VMEM((units, width), BF16),
            pltpu.VMEM((rows, units), F32),
            pltpu.VMEM((rows, lw), F32),
            pltpu.VMEM((rows, units), BF16),
            pltpu.SemaphoreType.DMA((PIECES,)),
            pltpu.SemaphoreType.DMA((PIECES,)),
        ],
        compiler_params=pltpu.CompilerParams(vmem_limit_bytes=VMEM_LIMIT),
        cost_estimate=COST,
        name="channel_mix",
    )(length, x, first, gains, mixes, accept, *pieces)


def hid_place():
    me = lax.axis_index("hid")
    y, z, c = me // (NZ * NC), me // NC % NZ, me % NC

    def at(yy, zz, cc):
        return {"hid": (yy * NZ + zz) * NC + cc}

    zu, zd = (z + 1) % NZ, (z + 3) % NZ
    peers = {"core": at(y, z, 1 - c), "up": at(y, zu, c), "down": at(y, zd, c), "y": at(1 - y, z, c)}
    return y, z, c, zu, (z + 2) % NZ, zd, peers


def meet(peers):
    barrier = pltpu.get_barrier_semaphore()
    for device in peers.values():
        pl.semaphore_signal(barrier, inc=1, device_id=device, device_id_type=MESH)
    pl.semaphore_wait(barrier, len(peers))


class Copies:
    def __init__(self, send, recv):
        self.send, self.recv, self.made = send, recv, []

    def start(self, src, dst, device):
        i = len(self.made)
        copy = pltpu.make_async_remote_copy(
            src_ref=src, dst_ref=dst, send_sem=self.send.at[i], recv_sem=self.recv.at[i],
            device_id=device, device_id_type=MESH,
        )
        copy.start()
        self.made.append(copy)
        return copy

    def finish(self):
        for copy in self.made:
            copy.wait_send()


def sum_terms(terms, acc, core_buf, pass_buf, near_buf, y_buf, copies, place):
    y, z, c, zu, z2, zd, peers = place
    half = terms.shape[3] // 2
    from_core = [
        copies.start(terms.at[1 - c, g], core_buf.at[g], peers["core"]) for g in (z2, zu, zd, z)
    ]

    def add_core(i, g):
        from_core[i].wait_recv()
        acc[g] = (terms[c, g].astype(F32) + core_buf[g].astype(F32)).astype(BF16)

    add_core(0, z2)
    first_up = copies.start(acc.at[z2, :, 0:half], pass_buf.at[0], peers["up"])
    first_down = copies.start(acc.at[z2, :, half : 2 * half], pass_buf.at[1], peers["down"])
    add_core(1, zu)
    add_core(2, zd)
    first_up.wait_recv()
    acc[zu, :, 0:half] = (acc[zu, :, 0:half].astype(F32) + pass_buf[0].astype(F32)).astype(BF16)
    second_up = copies.start(acc.at[zu], near_buf.at[0], peers["up"])
    first_down.wait_recv()
    acc[zd, :, half : 2 * half] = (
        acc[zd, :, half : 2 * half].astype(F32) + pass_buf[1].astype(F32)
    ).astype(BF16)
    second_down = copies.start(acc.at[zd], near_buf.at[1], peers["down"])
    add_core(3, z)
    second_up.wait_recv()
    second_down.wait_recv()

    def total_of(yy):
        return acc[z, yy].astype(F32) + near_buf[0, yy].astype(F32) + near_buf[1, yy].astype(F32)

    acc[z, 1 - y] = total_of(1 - y).astype(BF16)
    across = copies.start(acc.at[z, 1 - y], y_buf, peers["y"])
    own = total_of(y)
    across.wait_recv()
    return own + y_buf[...].astype(F32)


def sum_scratch(shape, copies):
    nc, nz, ny, rows, lw = shape
    return [
        pltpu.VMEM((nz, ny, rows, lw), BF16),
        pltpu.VMEM((nz, ny, rows, lw), BF16),
        pltpu.VMEM((2, ny, rows // 2, lw), BF16),
        pltpu.VMEM((2, ny, rows, lw), BF16),
        pltpu.VMEM((rows, lw), BF16),
        pltpu.SemaphoreType.DMA((copies,)),
        pltpu.SemaphoreType.DMA((copies,)),
    ]


def join_kernel(terms, x_ref, mid_ref, own_ref, acc, core_buf, pass_buf, near_buf, y_buf, send, recv):
    place = hid_place()
    y, z, c, zu, z2, zd, peers = place
    meet(peers)
    copies = Copies(send, recv)
    half = x_ref.shape[0] // 2
    total = sum_terms(terms, acc, core_buf, pass_buf, near_buf, y_buf, copies, place)
    own = (x_ref[...].astype(F32) + total).astype(BF16)
    own_ref[...] = own
    mid_ref[c, z, y] = own

    def pass_on(index, device):
        return copies.start(mid_ref.at[index], mid_ref.at[index], device)

    pass_on((c, z, y), peers["y"]).wait_recv()
    up = pass_on((c, z), peers["up"])
    down = pass_on((c, z), peers["down"])
    waits = [pass_on((c, z), peers["core"])]
    up.wait_recv()
    far = [pass_on((c, zd, slice(None), slice(0, half)), peers["up"])]
    waits.append(pass_on((c, zd), peers["core"]))
    down.wait_recv()
    far.append(pass_on((c, zu, slice(None), slice(half, 2 * half)), peers["down"]))
    waits.append(pass_on((c, zu), peers["core"]))
    for copy in far:
        copy.wait_recv()
    waits.append(pass_on((c, z2), peers["core"]))
    for copy in waits:
        copy.wait_recv()
    copies.finish()


def join(terms, x_share):
    rows, lw = x_share.shape
    shape = (NC, NZ, NY, rows, lw)
    return pl.pallas_call(
        join_kernel,
        out_shape=(jax.ShapeDtypeStruct(shape, BF16), jax.ShapeDtypeStruct((rows, lw), BF16)),
        in_specs=[VM, VM],
        out_specs=(VM, VM),
        scratch_shapes=sum_scratch(shape, 18),
        compiler_params=pltpu.CompilerParams(
            collective_id=0, has_side_effects=True, vmem_limit_bytes=VMEM_LIMIT
        ),
        cost_estimate=COST,
        name="join",
    )(terms.reshape(shape), x_share)


def close_kernel(
    len_ref, terms, own_ref, gate_ref, out_ref, acc, core_buf, pass_buf, near_buf, y_buf, send, recv
):
    place = hid_place()
    meet(place[-1])
    copies = Copies(send, recv)
    total = sum_terms(terms, acc, core_buf, pass_buf, near_buf, y_buf, copies, place)
    combined = own_ref[...].astype(F32) + gate_ref[...] * total
    row = lax.broadcasted_iota(jnp.int32, combined.shape, 0)
    out_ref[...] = jnp.where(row < len_ref[0], combined, 0.0).astype(BF16)
    copies.finish()


def close(length, terms, own, gate_rows):
    rows, lw = own.shape
    shape = (NC, NZ, NY, rows, lw)
    return pl.pallas_call(
        close_kernel,
        out_shape=jax.ShapeDtypeStruct((rows, lw), BF16),
        in_specs=[SM, VM, VM, VM],
        out_specs=VM,
        scratch_shapes=sum_scratch(shape, 9),
        compiler_params=pltpu.CompilerParams(
            collective_id=1, has_side_effects=True, vmem_limit_bytes=VMEM_LIMIT
        ),
        name="close",
    )(length, terms.reshape(shape), own, gate_rows)


def local(
    input_activations,
    prompt_extents,
    continuing_flags,
    owning_index,
    partition_arrangement,
    training_accept_pieces,
    training_lookup_pieces,
    training_content_pieces,
    normalizer_scales,
    prior_step_blends,
    forgetting_bias_vector,
    forgetting_left_lowrank,
    forgetting_right_lowrank,
    instant_emphasis,
    group_normalizer_scale,
    gating_projection,
    mixing_exit_projection,
    kept_summary_places,
    previous_normed_entries,
    feedforward_entry_proj,
    feedforward_exit_proj,
    feedforward_accept_proj,
):
    x = input_activations[0]
    rows, width = x.shape
    lw = mixing_exit_projection.shape[0]
    hid = lax.axis_size("hid")
    block_rows = training_accept_pieces.shape[0]
    resuming = continuing_flags[0]
    gains = normalizer_scales.astype(F32)
    carried = jnp.where(resuming == 1, previous_normed_entries[0].astype(F32), 0.0)

    own = jnp.stack([training_accept_pieces, training_lookup_pieces, training_content_pieces])
    own = own.astype(BF16).reshape(3, block_rows, hid, lw).transpose(2, 1, 0, 3)
    own = own.reshape(hid, block_rows, 3 * lw)
    swapped = lax.all_to_all(own, "hid", split_axis=0, concat_axis=0, tiled=True)
    fetched = lax.all_to_all(
        kept_summary_places[0, 0].astype(BF16).reshape(hid, -1, HEAD, HEAD),
        "hid", split_axis=0, concat_axis=0, tiled=True,
    )
    chosen = lax.dynamic_index_in_dim(fetched, owning_index[0], 0, keepdims=False)
    s0 = jnp.where(resuming == 1, chosen.astype(F32), 0.0)
    both = first_hop(jnp.concatenate([feedforward_entry_proj, feedforward_exit_proj]))
    pieces = third_hop(second_hop(first_hop(swapped)))
    pieces, both = lax.optimization_barrier((pieces, both))
    both = second_hop(both)

    terms, state, last_in = time_mix(
        partition_arrangement, prompt_extents, x, carried[0:1], gains, prior_step_blends,
        gating_projection, forgetting_left_lowrank, forgetting_right_lowrank,
        forgetting_bias_vector[None], instant_emphasis[None], group_normalizer_scale[None],
        s0, mixing_exit_projection, pieces,
    )
    terms, both = lax.optimization_barrier((terms, both))
    both = third_hop(both)
    x_share = lax.dynamic_slice_in_dim(x, lax.axis_index("hid") * lw, lw, 1)
    middle, own_middle = join(terms, x_share)
    out_terms, gate_rows, last_chan = channel_mix(
        prompt_extents, middle.reshape(hid, rows, lw), carried[1:2], gains, prior_step_blends,
        feedforward_accept_proj, both,
    )
    layer_out = close(prompt_extents, out_terms, own_middle, gate_rows)[None]
    shift_out = jnp.concatenate([last_in, last_chan]).astype(BF16)[None]
    return (layer_out, state[None], shift_out)


def solution(mesh):
    placed = (
        P("req", None, None),
        P("req"),
        P("req"),
        P("req"),
        P(),
        P(("req", "hid"), None),
        P(("req", "hid"), None),
        P(("req", "hid"), None),
        P(),
        P(),
        P("hid"),
        P(),
        P(None, "hid"),
        P("hid"),
        P("hid"),
        P(None, "hid"),
        P("hid", None),
        P("req", "hid", None, None, None),
        P("req", None, None),
        P(("req", "hid"), None),
        P(("req", "hid"), None),
        P(None, "hid"),
    )
    return jax.shard_map(
        local,
        mesh=mesh,
        in_specs=placed,
        out_specs=(P("req", None, "hid"), P("req", "hid", None, None), P("req", None, None)),
        check_vma=False,
    )
```

```python
from functools import partial

import jax
import jax.numpy as jnp
from jax import lax
from jax.experimental import pallas as pl
from jax.experimental.pallas import tpu as pltpu
from jax.sharding import PartitionSpec as P

HEAD = 64
CHUNK = 16
TILE = 64
PAIR = 128
KC = 512
VMEM_LIMIT = 58 * 1024 * 1024
F32 = jnp.float32
BF16 = jnp.bfloat16
MESH = pl.DeviceIdType.MESH
NY, NZ, NC = 2, 4, 2
NX, NW = 4, 2
PIECES = NX * NW
SPLIT = 9
COST = pl.CostEstimate(flops=40_000_000_000, bytes_accessed=40_000_000, transcendentals=0)
VM = pl.BlockSpec(memory_space=pltpu.VMEM)
SM = pl.BlockSpec(memory_space=pltpu.SMEM)
HB = pl.BlockSpec(memory_space=pl.ANY)


def nt_dot(a, b):
    return lax.dot_general(a, b, (((1,), (1,)), ((), ())), preferred_element_type=F32)


def tn_dot(a, b):
    return lax.dot_general(a, b, (((0,), (0,)), ((), ())), preferred_element_type=F32)


def nn_dot(a, b):
    return jnp.dot(a, b, preferred_element_type=F32)


def send(value, dx, dw):
    pairs = [(x * NW + w, (x + dx) % NX * NW + (w + dw) % NW) for x in range(NX) for w in range(NW)]
    return lax.ppermute(value, "req", pairs)


def second_hop(have):
    other = have[1]
    return have + [send(other, 1, 0), send(other, NX - 1, 0)]


def third_hop(have):
    return have + [send(have[2], 1, 0), send(have[5], NX - 1, 0)]


def group_columns(g, lw):
    block = (g % NY) * (NZ * NC) + (g // NY % NZ) * NC + g // (NY * NZ)
    return pl.ds(pl.multiple_of(block * lw, lw), lw)


def row_stats(part, count, rows, width, eps):
    def add_sum(c, total):
        return total + jnp.sum(part(c), axis=1, keepdims=True)

    def add_square(c, total):
        center = part(c) - mean
        return total + jnp.sum(center * center, axis=1, keepdims=True)

    zero = jnp.zeros((rows, 1), F32)
    mean = lax.fori_loop(0, count, add_sum, zero) / width
    var = lax.fori_loop(0, count, add_square, zero) / width
    return mean, 1.0 / jnp.sqrt(var + eps)


def normed_and_delta(part, first_ref, gain_ref, which, cols, mean, inv):
    normed = (part - mean) * inv * gain_ref[:, cols].astype(F32)[which : which + 1]
    before = pltpu.roll(normed, 1, 0)
    row = lax.broadcasted_iota(jnp.int32, normed.shape, 0)
    before = jnp.where(row == 0, first_ref[:, cols], before)
    return normed, before - normed


def pick_row(values, index):
    row = lax.broadcasted_iota(jnp.int32, values.shape, 0)
    return jnp.sum(jnp.where(row == index, values, 0.0), axis=0, keepdims=True)


def time_mix_kernel(
    perm_ref, len_ref, x_ref, first_ref, gain_ref, mix_ref, gating_ref, left_ref,
    right_ref, bias_ref, bonus_ref, gscale_ref, s0_ref, exit_ref, w_ref,
    terms_ref, state_ref, last_ref, share_ref,
    w_scr, acc, acc_low, acc_gate, logw_scr, prod_scr, gated_scr, st_scr, sem,
):
    rows, width = x_ref.shape
    block_rows = w_scr.shape[1] // 3
    lw = acc_gate.shape[1]


    def start(j, carry):
        pltpu.make_async_copy(w_ref.at[j], w_scr.at[perm_ref[j]], sem).start()
        return carry

    lax.fori_loop(0, w_scr.shape[0], start, 0)
    share_ref[...] = x_ref[:, pl.ds(pl.multiple_of(lax.axis_index("hid") * lw, lw), lw)]

    def part(c):
        return x_ref[:, pl.ds(pl.multiple_of(c * KC, KC), KC)].astype(F32)

    mean, inv = row_stats(part, width // KC, rows, width, 1e-05)
    acc[...] = jnp.zeros_like(acc)
    acc_low[...] = jnp.zeros_like(acc_low)
    acc_gate[...] = jnp.zeros_like(acc_gate)
    pltpu.make_async_copy(w_scr, w_scr, sem).wait()
    per = KC // block_rows

    def project(c, carry):
        cols = pl.ds(pl.multiple_of(c * KC, KC), KC)
        normed, delta = normed_and_delta(part(c), first_ref, gain_ref, 0, cols, mean, inv)
        last_ref[:, cols] = pick_row(normed, len_ref[0] - 1)
        mix = mix_ref[:, cols].astype(F32)

        def blend(m):
            return (normed + delta * mix[m : m + 1]).astype(BF16)

        for m in range(3):
            own_rows = slice(m * block_rows, (m + 1) * block_rows)
            wm = w_scr[pl.ds(c * per, per), own_rows, :].reshape(KC, lw)
            acc[:, m * lw : (m + 1) * lw] += nn_dot(blend(m), wm)
        acc_low[...] += nn_dot(blend(3), left_ref[cols, :])
        acc_gate[...] += nn_dot(blend(4), gating_ref[cols, :])
        return carry

    lax.fori_loop(0, width // KC, project, 0)
    length = len_ref[0]
    present = lax.broadcasted_iota(jnp.int32, (rows, lw), 0) < length
    low = jnp.tanh(acc_low[...]).astype(BF16)
    log_decay = -jnp.exp(bias_ref[...] + nn_dot(low, right_ref[...]))
    logw_scr[...] = jnp.where(present, log_decay, 0.0)
    acc[:, lw : 2 * lw] = jnp.where(present, acc[:, lw : 2 * lw], 0.0)

    pairs = lw // PAIR

    def same_head(size):
        a = lax.broadcasted_iota(jnp.int32, (size, size), 0) // HEAD
        b = lax.broadcasted_iota(jnp.int32, (size, size), 1) // HEAD
        return a == b

    pair_mask = same_head(PAIR)
    for p in range(pairs):
        two = s0_ref[:, p * PAIR : (p + 1) * PAIR]
        st_scr[p] = jnp.where(pair_mask, jnp.concatenate([two, two], axis=0), 0.0).T

    ones = jnp.where(same_head(lw), 1.0, 0.0).astype(BF16)
    slot = lax.broadcasted_iota(jnp.int32, (TILE, lw), 0) % CHUNK

    def head_sum(values):
        high = values.astype(BF16)
        rest = (values - high.astype(F32)).astype(BF16)
        return nn_dot(high, ones) + nn_dot(rest, ones)

    def tile_step(t, carry):
        here = pl.ds(pl.multiple_of(t * TILE, TILE), TILE)
        r = acc[here, 0:lw]
        k = acc[here, lw : 2 * lw]
        v = acc[here, 2 * lw : 3 * lw]
        decay = logw_scr[here, :]
        incl = decay
        step = 1
        while step < CHUNK:
            incl = incl + jnp.where(slot >= step, pltpu.roll(incl, step, 0), 0.0)
            step *= 2
        excl = incl - decay
        prod_scr[0:TILE, :] = (r * bonus_ref[...] * k).astype(BF16)
        for d in range(1, CHUNK):
            gap = jnp.minimum(excl - pltpu.roll(incl, d, 0), 0.0)
            term = jnp.where(slot >= d, r * pltpu.roll(k, d, 0) * jnp.exp(gap), 0.0)
            prod_scr[d * TILE : (d + 1) * TILE, :] = term.astype(BF16)
        scores = nn_dot(prod_scr[...], ones)
        out = scores[0:TILE] * v
        for d in range(1, CHUNK):
            out = out + scores[d * TILE : (d + 1) * TILE] * pltpu.roll(v, d, 0)
        rw = (r * jnp.exp(excl)).astype(BF16)
        vb = v.astype(BF16)
        pieces = []
        for c in range(TILE // CHUNK):
            lo, hi = c * CHUNK, (c + 1) * CHUNK
            closing = incl[hi - 1 : hi]
            kw = (k[lo:hi] * jnp.exp(closing - incl[lo:hi])).astype(BF16)
            fade = jnp.exp(closing)
            parts = []
            for p in range(pairs):
                a, b = p * PAIR, (p + 1) * PAIR
                st = st_scr[p]
                parts.append(nt_dot(rw[lo:hi, a:b], st.astype(BF16)))
                grown = tn_dot(vb[lo:hi, a:b], kw[:, a:b])
                st_scr[p] = st * fade[:, a:b] + jnp.where(pair_mask, grown, 0.0)
            pieces.append(jnp.concatenate(parts, axis=1))
        out = out + jnp.concatenate(pieces, axis=0)
        center = out - head_sum(out) * (1.0 / HEAD)
        spread = head_sum(center * center) * (1.0 / HEAD)
        grouped = center / jnp.sqrt(spread + 0.00064) * gscale_ref[...]
        g = acc_gate[here, :]
        gate = g / (1.0 + jnp.exp(-g))
        gated_scr[here, :] = (grouped * gate).astype(BF16)
        return carry

    lax.fori_loop(0, rows // TILE, tile_step, 0)
    for p in range(pairs):
        full = st_scr[p].T
        state_ref[2 * p] = full[0:HEAD, 0:HEAD]
        state_ref[2 * p + 1] = full[HEAD:PAIR, HEAD:PAIR]

    def leave(g, carry):
        terms_ref[g] = nn_dot(gated_scr[...], exit_ref[:, group_columns(g, lw)]).astype(BF16)
        return carry

    lax.fori_loop(0, width // lw, leave, 0)


def time_mix(perm, length, x, first, gains, mixes, gating, left, right, bias, bonus, gscale, s0, exit_w, w):
    rows, width = x.shape
    lw = gating.shape[1]
    return pl.pallas_call(
        time_mix_kernel,
        out_shape=(
            jax.ShapeDtypeStruct((width // lw, rows, lw), BF16),
            jax.ShapeDtypeStruct((lw // HEAD, HEAD, HEAD), F32),
            jax.ShapeDtypeStruct((1, width), F32),
            jax.ShapeDtypeStruct((rows, lw), BF16),
        ),
        in_specs=[SM, SM] + [VM] * 12 + [HB],
        out_specs=(VM, VM, VM, VM),
        scratch_shapes=[
            pltpu.VMEM(w.shape, BF16),
            pltpu.VMEM((rows, 3 * lw), F32),
            pltpu.VMEM((rows, left.shape[1]), F32),
            pltpu.VMEM((rows, lw), F32),
            pltpu.VMEM((rows, lw), F32),
            pltpu.VMEM((CHUNK * TILE, lw), BF16),
            pltpu.VMEM((rows, lw), BF16),
            pltpu.VMEM((lw // PAIR, PAIR, PAIR), F32),
            pltpu.SemaphoreType.DMA,
        ],
        compiler_params=pltpu.CompilerParams(vmem_limit_bytes=VMEM_LIMIT),
        cost_estimate=COST,
        name="time_mix",
    )(perm, length, x, first, gains, mixes, gating, left, right, bias, bonus, gscale, s0, exit_w, w)


def channel_mix_kernel(
    len_ref, x_ref, first_ref, gain_ref, mix_ref, accept_ref, *refs,
):
    pieces = refs[:PIECES]
    terms_ref, gate_ref, last_ref = refs[PIECES : PIECES + 3]
    key_scr, value_scr, inner, acc_gate, hidden, key_sems, value_sems = refs[PIECES + 3 :]
    groups, rows, lw = x_ref.shape
    units = pieces[0].shape[0] // 2

    def fetch(begin, scr, sems):
        copies = [
            pltpu.make_async_copy(
                piece.at[pl.ds(begin, units)], scr.at[pl.ds(i * units, units)], sems.at[i]
            )
            for i, piece in enumerate(pieces)
        ]
        for copy in copies:
            copy.start()
        return copies

    key_copies = fetch(0, key_scr, key_sems)
    value_copies = fetch(units, value_scr, value_sems)

    def part(g):
        return x_ref[g].astype(F32)

    mean, inv = row_stats(part, groups, rows, groups * lw, 1e-05)
    inner[...] = jnp.zeros_like(inner)
    acc_gate[...] = jnp.zeros_like(acc_gate)
    for copy in key_copies:
        copy.wait()

    def project(g, carry):
        cols = group_columns(g, lw)
        normed, delta = normed_and_delta(part(g), first_ref, gain_ref, 1, cols, mean, inv)
        last_ref[:, cols] = pick_row(normed, len_ref[0] - 1)
        mix = mix_ref[:, cols].astype(F32)
        inner[...] += nt_dot((normed + delta * mix[5:6]).astype(BF16), key_scr[:, cols])
        acc_gate[...] += nn_dot((normed + delta * mix[6:7]).astype(BF16), accept_ref[cols, :])
        return carry

    lax.fori_loop(0, groups, project, 0)
    positive = jnp.maximum(inner[...], 0.0)
    hidden[...] = (positive * positive).astype(BF16)
    gate_ref[...] = jax.nn.sigmoid(acc_gate[...])
    for copy in value_copies:
        copy.wait()

    def leave(g, carry):
        terms_ref[g] = nn_dot(hidden[...], value_scr[:, group_columns(g, lw)]).astype(BF16)
        return carry

    lax.fori_loop(0, groups, leave, 0)


def channel_mix(length, x, first, gains, mixes, accept, pieces):
    groups, rows, lw = x.shape
    units = PIECES * pieces[0].shape[0] // 2
    width = groups * lw
    return pl.pallas_call(
        channel_mix_kernel,
        out_shape=(
            jax.ShapeDtypeStruct((groups, rows, lw), BF16),
            jax.ShapeDtypeStruct((rows, lw), F32),
            jax.ShapeDtypeStruct((1, groups * lw), F32),
        ),
        in_specs=[SM] + [VM] * 5 + [HB] * PIECES,
        out_specs=(VM, VM, VM),
        scratch_shapes=[
            pltpu.VMEM((units, width), BF16),
            pltpu.VMEM((units, width), BF16),
            pltpu.VMEM((rows, units), F32),
            pltpu.VMEM((rows, lw), F32),
            pltpu.VMEM((rows, units), BF16),
            pltpu.SemaphoreType.DMA((PIECES,)),
            pltpu.SemaphoreType.DMA((PIECES,)),
        ],
        compiler_params=pltpu.CompilerParams(vmem_limit_bytes=VMEM_LIMIT),
        cost_estimate=COST,
        name="channel_mix",
    )(length, x, first, gains, mixes, accept, *pieces)


def hid_place():
    me = lax.axis_index("hid")
    y, z, c = me // (NZ * NC), me // NC % NZ, me % NC

    def at(yy, zz, cc):
        return {"hid": (yy * NZ + zz) * NC + cc}

    zu, zd = (z + 1) % NZ, (z + 3) % NZ
    peers = {"core": at(y, z, 1 - c), "up": at(y, zu, c), "down": at(y, zd, c), "y": at(1 - y, z, c)}
    return y, z, c, zu, (z + 2) % NZ, zd, peers


def meet(peers):
    barrier = pltpu.get_barrier_semaphore()
    for device in peers.values():
        pl.semaphore_signal(barrier, inc=1, device_id=device, device_id_type=MESH)
    pl.semaphore_wait(barrier, len(peers))


class Copies:
    def __init__(self, send, recv):
        self.send, self.recv, self.made = send, recv, []

    def start(self, src, dst, device):
        i = len(self.made)
        copy = pltpu.make_async_remote_copy(
            src_ref=src, dst_ref=dst, send_sem=self.send.at[i], recv_sem=self.recv.at[i],
            device_id=device, device_id_type=MESH,
        )
        copy.start()
        self.made.append(copy)
        return copy

    def finish(self):
        for copy in self.made:
            copy.wait_send()


def sum_terms(terms, acc, core_buf, pass_a, near_a, y_a, pass_b, near_b, y_b, copies, place):
    y, z, c, zu, z2, zd, peers = place
    quarter = terms.shape[3] // 4
    a, a0, a1 = slice(0, 2 * quarter), slice(0, quarter), slice(quarter, 2 * quarter)
    b, b0, b1 = (slice(p.start + 2 * quarter, p.stop + 2 * quarter) for p in (a, a0, a1))
    groups = (z2, zu, zd, z)
    from_core = [copies.start(terms.at[1 - c, g], core_buf.at[g], peers["core"]) for g in groups]

    def add(index, values):
        acc[index] = (acc[index].astype(F32) + values.astype(F32)).astype(BF16)

    def add_core(i):
        g = groups[i]
        from_core[i].wait_recv()
        acc[g] = (terms[c, g].astype(F32) + core_buf[g].astype(F32)).astype(BF16)
        return copies.start(acc.at[g, 1 - y, b], y_b.at[g], peers["y"])

    across_b = [add_core(0)]
    pass_up = copies.start(acc.at[z2, :, a0], pass_a.at[0], peers["up"])
    pass_down = copies.start(acc.at[z2, :, a1], pass_a.at[1], peers["down"])
    across_b += [add_core(1), add_core(2)]
    pass_up.wait_recv()
    add((zu, slice(None), a0), pass_a[0])
    near_up = copies.start(acc.at[zu, :, a], near_a.at[0], peers["up"])
    pass_down.wait_recv()
    add((zd, slice(None), a1), pass_a[1])
    near_down = copies.start(acc.at[zd, :, a], near_a.at[1], peers["down"])
    across_b.append(add_core(3))
    across_b[0].wait_recv()
    add((z2, y, b), y_b[z2])
    pass_b_up = copies.start(acc.at[z2, y, b0], pass_b.at[0], peers["up"])
    pass_b_down = copies.start(acc.at[z2, y, b1], pass_b.at[1], peers["down"])
    across_b[1].wait_recv()
    add((zu, y, b), y_b[zu])
    across_b[2].wait_recv()
    add((zd, y, b), y_b[zd])
    near_up.wait_recv()
    near_down.wait_recv()

    def total_a(yy):
        return acc[z, yy, a].astype(F32) + near_a[0, yy].astype(F32) + near_a[1, yy].astype(F32)

    acc[z, 1 - y, a] = total_a(1 - y).astype(BF16)
    across_a = copies.start(acc.at[z, 1 - y, a], y_a, peers["y"])
    pass_b_up.wait_recv()
    add((zu, y, b0), pass_b[0])
    near_b_up = copies.start(acc.at[zu, y, b], near_b.at[0], peers["up"])
    pass_b_down.wait_recv()
    add((zd, y, b1), pass_b[1])
    near_b_down = copies.start(acc.at[zd, y, b], near_b.at[1], peers["down"])
    across_a.wait_recv()
    upper = total_a(y) + y_a[...].astype(F32)
    across_b[3].wait_recv()
    lower = acc[z, y, b].astype(F32) + y_b[z].astype(F32)
    near_b_up.wait_recv()
    near_b_down.wait_recv()
    lower = lower + near_b[0].astype(F32) + near_b[1].astype(F32)
    return (a, upper), (b, lower)


SUM_COPIES, COLLECT_COPIES = 17, 17


def sum_scratch(shape, copies):
    nc, nz, ny, rows, lw = shape
    half, quarter = rows // 2, rows // 4
    return [
        pltpu.VMEM((nz, ny, rows, lw), BF16),
        pltpu.VMEM((nz, ny, rows, lw), BF16),
        pltpu.VMEM((2, ny, quarter, lw), BF16),
        pltpu.VMEM((2, ny, half, lw), BF16),
        pltpu.VMEM((half, lw), BF16),
        pltpu.VMEM((2, quarter, lw), BF16),
        pltpu.VMEM((2, half, lw), BF16),
        pltpu.VMEM((nz, half, lw), BF16),
        pltpu.SemaphoreType.DMA((copies,)),
        pltpu.SemaphoreType.DMA((copies,)),
    ]


def spread_kernel(
    owner_ref, flag_ref, rec_ref, key_ref, val_ref, kept_ref,
    w_ref, s0_ref,
    own, got, own_state, got_state, local_sem, sems, state_sems, send_w, recv_w,
):
    me, at = lax.axis_index("hid"), lax.axis_index("req")
    x, w = at // NW, at % NW
    hid, _, lw = own.shape
    block_rows = rec_ref.shape[0]
    heads = lw // HEAD
    peers = {
        "mate": {"req": x * NW + 1 - w},
        "up": {"req": (x + 1) % NX * NW + w},
        "down": {"req": (x + NX - 1) % NX * NW + w},
    }
    barrier = pltpu.get_barrier_semaphore()
    for i in range(1, hid):
        pl.semaphore_signal(
            barrier, inc=1, device_id={"hid": (me + i) % hid}, device_id_type=MESH
        )
    for device in peers.values():
        pl.semaphore_signal(barrier, inc=1, device_id=device, device_id_type=MESH)

    def fill(h):
        cols = pl.ds(pl.multiple_of(h * lw, lw), lw)
        for m, ref in enumerate((rec_ref, key_ref, val_ref)):
            own[h, m * block_rows : (m + 1) * block_rows, :] = ref[:, cols].astype(BF16)

    def fill_state(h):
        state = jnp.concatenate([kept_ref[h * heads + i] for i in range(heads)], axis=1)
        own_state[h] = state.astype(BF16)

    def swap(i, src, dst, sems):
        to = (me + i) % hid
        return pltpu.make_async_remote_copy(
            src_ref=src.at[to], dst_ref=dst.at[me], send_sem=sems.at[0, i - 1],
            recv_sem=sems.at[1, i - 1], device_id={"hid": to}, device_id_type=MESH,
        )

    def fill_and_send(i, carry):
        fill((me + i) % hid)
        swap(i, own, got, sems).start()
        return carry

    def fill_and_send_state(i, carry):
        fill_state((me + i) % hid)
        swap(i, own_state, got_state, state_sems).start()
        return carry

    def arrive(i, carry):
        swap(i, own, got, sems).wait_recv()
        return carry

    def finish(i, carry):
        swap(i, own, got, sems).wait_send()
        swap(i, own_state, got_state, state_sems).wait()
        return carry

    pl.semaphore_wait(barrier, hid - 1 + len(peers))
    lax.fori_loop(1, hid, fill_and_send, 0)
    fill(me)
    got[me] = own[me]
    lax.fori_loop(1, hid, arrive, 0)
    copies = Copies(send_w, recv_w)
    mate = x * NW + 1 - w
    before, after = (x + NX - 1) % NX * NW, (x + 1) % NX * NW
    a, b = slice(0, SPLIT), slice(SPLIT, hid)
    b0, b1 = slice(SPLIT, (SPLIT + hid) // 2), slice((SPLIT + hid) // 2, hid)
    keep = pltpu.make_async_copy(got, w_ref.at[at], local_sem)

    def pass_on(index, rows, device, first=False):
        here = w_ref.at[index, rows]
        return copies.start(got.at[rows] if first else here, here, peers[device])

    a_up, a_down = pass_on(at, a, "up", True), pass_on(at, a, "down", True)
    a_mate = pass_on(at, a, "mate", True)
    b_up, b_down = pass_on(at, b, "up", True), pass_on(at, b, "down", True)
    b_mates = [pass_on(at, b, "mate", True)]
    keep.start()
    fill_state(me)
    got_state[me] = own_state[me]
    lax.fori_loop(1, hid, fill_and_send_state, 0)
    a_up.wait_recv()
    far_up = pass_on(before + w, a, "up")
    a_mate.wait_recv()
    mate_up, mate_down = pass_on(mate, a, "up"), pass_on(mate, a, "down")
    a_down.wait_recv()
    b_up.wait_recv()
    b_mates.append(pass_on(before + w, b, "mate"))
    far_b_up = pass_on(before + w, b0, "up")
    b_down.wait_recv()
    far_b_down = pass_on(after + w, b1, "down")
    b_mates.append(pass_on(after + w, b, "mate"))
    mate_down.wait_recv()
    far_down = pass_on(after + 1 - w, a, "down")
    far_b_up.wait_recv()
    far_b_down.wait_recv()
    b_mates.append(pass_on((x + 2) % NX * NW + w, b, "mate"))
    lax.fori_loop(1, hid, finish, 0)
    s0_ref[...] = jnp.where(flag_ref[0] == 1, got_state[owner_ref[0]].astype(F32), 0.0)
    for copy in [mate_up, far_up, far_down] + b_mates:
        copy.wait_recv()
    keep.wait()
    copies.finish()


def spread(owner, flag, rec, key, val, kept, hid):
    block_rows, width = rec.shape
    lw = width // hid
    req = NX * NW
    return pl.pallas_call(
        spread_kernel,
        out_shape=(
            jax.ShapeDtypeStruct((req, hid, 3 * block_rows, lw), BF16),
            jax.ShapeDtypeStruct((HEAD, lw), F32),
        ),
        in_specs=[SM, SM, VM, VM, VM, VM],
        out_specs=(HB, VM),
        scratch_shapes=[
            pltpu.VMEM((hid, 3 * block_rows, lw), BF16),
            pltpu.VMEM((hid, 3 * block_rows, lw), BF16),
            pltpu.VMEM((hid, HEAD, lw), BF16),
            pltpu.VMEM((hid, HEAD, lw), BF16),
            pltpu.SemaphoreType.DMA,
            pltpu.SemaphoreType.DMA((2, hid - 1)),
            pltpu.SemaphoreType.DMA((2, hid - 1)),
            pltpu.SemaphoreType.DMA((15,)),
            pltpu.SemaphoreType.DMA((15,)),
        ],
        compiler_params=pltpu.CompilerParams(
            collective_id=2, has_side_effects=True, vmem_limit_bytes=VMEM_LIMIT
        ),
        cost_estimate=COST,
        name="spread",
    )(owner, flag, rec, key, val, kept)


def join_kernel(terms, x_ref, mid_ref, own_ref, *scratch):
    place = hid_place()
    y, z, c, zu, z2, zd, peers = place
    meet(peers)
    copies = Copies(*scratch[-2:])
    quarter = x_ref.shape[0] // 4
    every = slice(None)
    a, a0, a1 = slice(0, 2 * quarter), slice(0, quarter), slice(quarter, 2 * quarter)
    b, b0, b1 = (slice(p.start + 2 * quarter, p.stop + 2 * quarter) for p in (a, a0, a1))
    for rows, total in sum_terms(terms, *scratch[:-2], copies, place):
        own = (x_ref[rows].astype(F32) + total).astype(BF16)
        own_ref[rows] = own
        mid_ref[c, z, y, rows] = own

    def pass_on(device, *index):
        return copies.start(mid_ref.at[index], mid_ref.at[index], peers[device])

    across_a = pass_on("y", c, z, y, a)
    near_b_up = pass_on("up", c, z, y, b)
    near_b_down = pass_on("down", c, z, y, b)
    across_b = [pass_on("y", c, z, y, b)]
    across_a.wait_recv()
    near_a_up = pass_on("up", c, z, every, a)
    near_a_down = pass_on("down", c, z, every, a)
    near_b_up.wait_recv()
    far_b_up = pass_on("up", c, zd, y, b0)
    across_b.append(pass_on("y", c, zd, y, b))
    near_b_down.wait_recv()
    far_b_down = pass_on("down", c, zu, y, b1)
    across_b.append(pass_on("y", c, zu, y, b))
    near_a_up.wait_recv()
    far_a_up = pass_on("up", c, zd, every, a0)
    near_a_down.wait_recv()
    far_a_down = pass_on("down", c, zu, every, a1)
    far_b_up.wait_recv()
    far_b_down.wait_recv()
    across_b.append(pass_on("y", c, z2, y, b))
    to_core = []
    for i, g in enumerate((z, zd, zu)):
        across_b[i].wait_recv()
        to_core.append(pass_on("core", c, g))
    far_a_up.wait_recv()
    far_a_down.wait_recv()
    across_b[3].wait_recv()
    to_core.append(pass_on("core", c, z2))
    for copy in to_core:
        copy.wait_recv()
    copies.finish()


def join(terms, x_share):
    rows, lw = x_share.shape
    shape = (NC, NZ, NY, rows, lw)
    return pl.pallas_call(
        join_kernel,
        out_shape=(jax.ShapeDtypeStruct(shape, BF16), jax.ShapeDtypeStruct((rows, lw), BF16)),
        in_specs=[VM, VM],
        out_specs=(VM, VM),
        scratch_shapes=sum_scratch(shape, SUM_COPIES + COLLECT_COPIES),
        compiler_params=pltpu.CompilerParams(
            collective_id=0, has_side_effects=True, vmem_limit_bytes=VMEM_LIMIT
        ),
        cost_estimate=COST,
        name="join",
    )(terms.reshape(shape), x_share)


def close_kernel(len_ref, terms, own_ref, gate_ref, out_ref, *scratch):
    place = hid_place()
    meet(place[-1])
    copies = Copies(*scratch[-2:])
    for rows, total in sum_terms(terms, *scratch[:-2], copies, place):
        combined = own_ref[rows].astype(F32) + gate_ref[rows] * total
        row = lax.broadcasted_iota(jnp.int32, combined.shape, 0) + rows.start
        out_ref[rows] = jnp.where(row < len_ref[0], combined, 0.0).astype(BF16)
    copies.finish()


def close(length, terms, own, gate_rows):
    rows, lw = own.shape
    shape = (NC, NZ, NY, rows, lw)
    return pl.pallas_call(
        close_kernel,
        out_shape=jax.ShapeDtypeStruct((rows, lw), BF16),
        in_specs=[SM, VM, VM, VM],
        out_specs=VM,
        scratch_shapes=sum_scratch(shape, SUM_COPIES),
        compiler_params=pltpu.CompilerParams(
            collective_id=1, has_side_effects=True, vmem_limit_bytes=VMEM_LIMIT
        ),
        name="close",
    )(length, terms.reshape(shape), own, gate_rows)


def local(
    input_activations,
    prompt_extents,
    continuing_flags,
    owning_index,
    partition_arrangement,
    training_accept_pieces,
    training_lookup_pieces,
    training_content_pieces,
    normalizer_scales,
    prior_step_blends,
    forgetting_bias_vector,
    forgetting_left_lowrank,
    forgetting_right_lowrank,
    instant_emphasis,
    group_normalizer_scale,
    gating_projection,
    mixing_exit_projection,
    kept_summary_places,
    previous_normed_entries,
    feedforward_entry_proj,
    feedforward_exit_proj,
    feedforward_accept_proj,
):
    x = input_activations[0]
    rows, width = x.shape
    lw = mixing_exit_projection.shape[0]
    hid = lax.axis_size("hid")
    block_rows = training_accept_pieces.shape[0]
    resuming = continuing_flags[0]
    gains = normalizer_scales.astype(F32)
    carried = jnp.where(resuming == 1, previous_normed_entries[0].astype(F32), 0.0)

    both = jnp.concatenate([feedforward_entry_proj, feedforward_exit_proj])
    both = [both, send(both, 0, 1), send(both, 1, 0), send(both, NX - 1, 0)]
    w, s0 = spread(
        owning_index, continuing_flags, training_accept_pieces, training_lookup_pieces,
        training_content_pieces, kept_summary_places[0, 0], hid,
    )
    both, w = lax.optimization_barrier((both, w))
    both = second_hop(both)
    w = w.reshape(-1, 3 * block_rows, lw)
    terms, state, last_in, x_share = time_mix(
        partition_arrangement, prompt_extents, x, carried[0:1], gains, prior_step_blends,
        gating_projection, forgetting_left_lowrank, forgetting_right_lowrank,
        forgetting_bias_vector[None], instant_emphasis[None], group_normalizer_scale[None],
        s0, mixing_exit_projection, w,
    )
    terms, both = lax.optimization_barrier((terms, both))
    both = third_hop(both)
    middle, own_middle = join(terms, x_share)
    out_terms, gate_rows, last_chan = channel_mix(
        prompt_extents, middle.reshape(hid, rows, lw), carried[1:2], gains, prior_step_blends,
        feedforward_accept_proj, both,
    )
    layer_out = close(prompt_extents, out_terms, own_middle, gate_rows)[None]
    shift_out = jnp.concatenate([last_in, last_chan]).astype(BF16)[None]
    return (layer_out, state[None], shift_out)


def solution(mesh):
    placed = (
        P("req", None, None),
        P("req"),
        P("req"),
        P("req"),
        P(),
        P(("req", "hid"), None),
        P(("req", "hid"), None),
        P(("req", "hid"), None),
        P(),
        P(),
        P("hid"),
        P(),
        P(None, "hid"),
        P("hid"),
        P("hid"),
        P(None, "hid"),
        P("hid", None),
        P("req", "hid", None, None, None),
        P("req", None, None),
        P(("req", "hid"), None),
        P(("req", "hid"), None),
        P(None, "hid"),
    )
    return jax.shard_map(
        local,
        mesh=mesh,
        in_specs=placed,
        out_specs=(P("req", None, "hid"), P("req", "hid", None, None), P("req", None, None)),
        check_vma=False,
    )
```

```python
from functools import partial

import jax
import jax.numpy as jnp
from jax import lax
from jax.experimental import pallas as pl
from jax.experimental.pallas import tpu as pltpu
from jax.sharding import PartitionSpec as P

HEAD = 64
CHUNK = 16
TILE = 64
PAIR = 128
KC = 512
GROUPS_IN, GROUPS_OUT = 4, 4
VMEM_LIMIT = 58 * 1024 * 1024
F32 = jnp.float32
BF16 = jnp.bfloat16
MESH = pl.DeviceIdType.MESH
NY, NZ, NC = 2, 4, 2
NX, NW = 4, 2
PIECES = NX * NW
SPLIT = 9
COST = pl.CostEstimate(flops=40_000_000_000, bytes_accessed=40_000_000, transcendentals=0)
VM = pl.BlockSpec(memory_space=pltpu.VMEM)
SM = pl.BlockSpec(memory_space=pltpu.SMEM)
HB = pl.BlockSpec(memory_space=pl.ANY)


def nt_dot(a, b):
    return lax.dot_general(a, b, (((1,), (1,)), ((), ())), preferred_element_type=F32)


def tn_dot(a, b):
    return lax.dot_general(a, b, (((0,), (0,)), ((), ())), preferred_element_type=F32)


def nn_dot(a, b):
    return jnp.dot(a, b, preferred_element_type=F32)


def send(value, dx, dw):
    pairs = [(x * NW + w, (x + dx) % NX * NW + (w + dw) % NW) for x in range(NX) for w in range(NW)]
    return lax.ppermute(value, "req", pairs)


def group_columns(g, lw):
    block = (g % NY) * (NZ * NC) + (g // NY % NZ) * NC + g // (NY * NZ)
    return pl.ds(pl.multiple_of(block * lw, lw), lw)


def row_stats(part, count, rows, width, eps):
    def add_sum(c, total):
        return total + jnp.sum(part(c), axis=1, keepdims=True)

    def add_square(c, total):
        center = part(c) - mean
        return total + jnp.sum(center * center, axis=1, keepdims=True)

    zero = jnp.zeros((rows, 1), F32)
    mean = lax.fori_loop(0, count, add_sum, zero) / width
    var = lax.fori_loop(0, count, add_square, zero) / width
    return mean, 1.0 / jnp.sqrt(var + eps)


def normed_and_delta(part, flag_ref, first_ref, gain_ref, which, cols, mean, inv):
    normed = (part - mean) * inv * gain_ref[:, cols].astype(F32)[which : which + 1]
    before = pltpu.roll(normed, 1, 0)
    row = lax.broadcasted_iota(jnp.int32, normed.shape, 0)
    saved = first_ref[:, cols].astype(F32)[which : which + 1]
    before = jnp.where(row == 0, jnp.where(flag_ref[0] == 1, saved, 0.0), before)
    return normed, before - normed


def pick_row(values, index):
    row = lax.broadcasted_iota(jnp.int32, values.shape, 0)
    return jnp.sum(jnp.where(row == index, values, 0.0), axis=0, keepdims=True)


def time_mix_kernel(
    perm_ref, len_ref, flag_ref, x_ref, first_ref, gain_ref, mix_ref, gating_ref, left_ref,
    right_ref, bias_ref, bonus_ref, gscale_ref, s0_ref, exit_ref, w_ref,
    terms_ref, state_ref, last_ref, share_ref,
    w_scr, acc, acc_low, acc_gate, logw_scr, prod_scr, gated_scr, st_scr, sem,
):
    rows, width = x_ref.shape
    block_rows = w_scr.shape[1] // 3
    lw = acc_gate.shape[1]


    def start(j, carry):
        pltpu.make_async_copy(w_ref.at[j], w_scr.at[perm_ref[j]], sem).start()
        return carry

    lax.fori_loop(0, w_scr.shape[0], start, 0)
    share_ref[...] = x_ref[:, pl.ds(pl.multiple_of(lax.axis_index("hid") * lw, lw), lw)]

    def part(c):
        return x_ref[:, pl.ds(pl.multiple_of(c * KC, KC), KC)].astype(F32)

    mean, inv = row_stats(part, width // KC, rows, width, 1e-05)
    acc[...] = jnp.zeros_like(acc)
    acc_low[...] = jnp.zeros_like(acc_low)
    acc_gate[...] = jnp.zeros_like(acc_gate)
    pltpu.make_async_copy(w_scr, w_scr, sem).wait()
    per = KC // block_rows

    def project(c, carry):
        cols = pl.ds(pl.multiple_of(c * KC, KC), KC)
        normed, delta = normed_and_delta(part(c), flag_ref, first_ref, gain_ref, 0, cols, mean, inv)
        last_ref[:, cols] = pick_row(normed, len_ref[0] - 1)
        mix = mix_ref[:, cols].astype(F32)

        def blend(m):
            return (normed + delta * mix[m : m + 1]).astype(BF16)

        for m in range(3):
            own_rows = slice(m * block_rows, (m + 1) * block_rows)
            wm = w_scr[pl.ds(c * per, per), own_rows, :].reshape(KC, lw)
            acc[:, m * lw : (m + 1) * lw] += nn_dot(blend(m), wm)
        acc_low[...] += nn_dot(blend(3), left_ref[cols, :])
        acc_gate[...] += nn_dot(blend(4), gating_ref[cols, :])
        return carry

    lax.fori_loop(0, width // KC, project, 0)
    length = len_ref[0]
    present = lax.broadcasted_iota(jnp.int32, (rows, lw), 0) < length
    low = jnp.tanh(acc_low[...]).astype(BF16)
    log_decay = -jnp.exp(bias_ref[...] + nn_dot(low, right_ref[...]))
    logw_scr[...] = jnp.where(present, log_decay, 0.0)
    acc[:, lw : 2 * lw] = jnp.where(present, acc[:, lw : 2 * lw], 0.0)

    pairs = lw // PAIR

    def same_head(size):
        a = lax.broadcasted_iota(jnp.int32, (size, size), 0) // HEAD
        b = lax.broadcasted_iota(jnp.int32, (size, size), 1) // HEAD
        return a == b

    pair_mask = same_head(PAIR)
    for p in range(pairs):
        two = s0_ref[:, p * PAIR : (p + 1) * PAIR]
        st_scr[p] = jnp.where(pair_mask, jnp.concatenate([two, two], axis=0), 0.0).T

    ones = jnp.where(same_head(lw), 1.0, 0.0).astype(BF16)
    slot = lax.broadcasted_iota(jnp.int32, (TILE, lw), 0) % CHUNK

    def head_sum(values):
        high = values.astype(BF16)
        rest = (values - high.astype(F32)).astype(BF16)
        return nn_dot(high, ones) + nn_dot(rest, ones)

    def tile_step(t, carry):
        here = pl.ds(pl.multiple_of(t * TILE, TILE), TILE)
        r = acc[here, 0:lw]
        k = acc[here, lw : 2 * lw]
        v = acc[here, 2 * lw : 3 * lw]
        decay = logw_scr[here, :]
        incl = decay
        step = 1
        while step < CHUNK:
            incl = incl + jnp.where(slot >= step, pltpu.roll(incl, step, 0), 0.0)
            step *= 2
        excl = incl - decay
        prod_scr[0:TILE, :] = (r * bonus_ref[...] * k).astype(BF16)
        for d in range(1, CHUNK):
            gap = jnp.minimum(excl - pltpu.roll(incl, d, 0), 0.0)
            term = jnp.where(slot >= d, r * pltpu.roll(k, d, 0) * jnp.exp(gap), 0.0)
            prod_scr[d * TILE : (d + 1) * TILE, :] = term.astype(BF16)
        scores = nn_dot(prod_scr[...], ones)
        out = scores[0:TILE] * v
        for d in range(1, CHUNK):
            out = out + scores[d * TILE : (d + 1) * TILE] * pltpu.roll(v, d, 0)
        rw = (r * jnp.exp(excl)).astype(BF16)
        vb = v.astype(BF16)
        pieces = []
        for c in range(TILE // CHUNK):
            lo, hi = c * CHUNK, (c + 1) * CHUNK
            closing = incl[hi - 1 : hi]
            kw = (k[lo:hi] * jnp.exp(closing - incl[lo:hi])).astype(BF16)
            fade = jnp.exp(closing)
            parts = []
            for p in range(pairs):
                a, b = p * PAIR, (p + 1) * PAIR
                st = st_scr[p]
                parts.append(nt_dot(rw[lo:hi, a:b], st.astype(BF16)))
                grown = tn_dot(vb[lo:hi, a:b], kw[:, a:b])
                st_scr[p] = st * fade[:, a:b] + jnp.where(pair_mask, grown, 0.0)
            pieces.append(jnp.concatenate(parts, axis=1))
        out = out + jnp.concatenate(pieces, axis=0)
        center = out - head_sum(out) * (1.0 / HEAD)
        spread = head_sum(center * center) * (1.0 / HEAD)
        grouped = center / jnp.sqrt(spread + 0.00064) * gscale_ref[...]
        g = acc_gate[here, :]
        gate = g / (1.0 + jnp.exp(-g))
        gated_scr[here, :] = (grouped * gate).astype(BF16)
        return carry

    lax.fori_loop(0, rows // TILE, tile_step, 0)
    for p in range(pairs):
        full = st_scr[p].T
        state_ref[2 * p] = full[0:HEAD, 0:HEAD]
        state_ref[2 * p + 1] = full[HEAD:PAIR, HEAD:PAIR]

    def leave(g, carry):
        terms_ref[g] = nn_dot(gated_scr[...], exit_ref[:, group_columns(g, lw)]).astype(BF16)
        return carry

    lax.fori_loop(0, width // lw, leave, 0)


def time_mix(perm, length, flag, x, first, gains, mixes, gating, left, right, bias, bonus, gscale, s0, exit_w, w):
    rows, width = x.shape
    lw = gating.shape[1]
    return pl.pallas_call(
        time_mix_kernel,
        out_shape=(
            jax.ShapeDtypeStruct((width // lw, rows, lw), BF16),
            jax.ShapeDtypeStruct((lw // HEAD, HEAD, HEAD), F32),
            jax.ShapeDtypeStruct((1, width), F32),
            jax.ShapeDtypeStruct((rows, lw), BF16),
        ),
        in_specs=[SM, SM, SM] + [VM] * 12 + [HB],
        out_specs=(VM, VM, VM, VM),
        scratch_shapes=[
            pltpu.VMEM(w.shape, BF16),
            pltpu.VMEM((rows, 3 * lw), F32),
            pltpu.VMEM((rows, left.shape[1]), F32),
            pltpu.VMEM((rows, lw), F32),
            pltpu.VMEM((rows, lw), F32),
            pltpu.VMEM((CHUNK * TILE, lw), BF16),
            pltpu.VMEM((rows, lw), BF16),
            pltpu.VMEM((lw // PAIR, PAIR, PAIR), F32),
            pltpu.SemaphoreType.DMA,
        ],
        compiler_params=pltpu.CompilerParams(vmem_limit_bytes=VMEM_LIMIT),
        cost_estimate=COST,
        name="time_mix",
    )(perm, length, flag, x, first, gains, mixes, gating, left, right, bias, bonus, gscale, s0, exit_w, w)


def channel_mix_kernel(
    len_ref, flag_ref, last_in_ref, x_ref, first_ref, gain_ref, mix_ref, accept_ref, *refs,
):
    entry_ref, exit_ref, *pairs = refs[: PIECES + 1]
    terms_ref, gate_ref, shift_ref = refs[PIECES + 1 : PIECES + 4]
    key_scr, value_scr, inner, acc_gate, hidden, key_sems, value_sems = refs[PIECES + 4 :]
    groups, rows, lw = x_ref.shape
    units = entry_ref.shape[0]

    def fetch(own, begin, scr, sems):
        pieces = [own] + [piece.at[pl.ds(begin, units)] for piece in pairs]
        copies = [
            pltpu.make_async_copy(piece, scr.at[pl.ds(i * units, units)], sems.at[i])
            for i, piece in enumerate(pieces)
        ]
        for copy in copies:
            copy.start()
        return copies

    key_copies = fetch(entry_ref, 0, key_scr, key_sems)
    value_copies = fetch(exit_ref, units, value_scr, value_sems)

    def part(g):
        return x_ref[g].astype(F32)

    mean, inv = row_stats(part, groups, rows, groups * lw, 1e-05)
    inner[...] = jnp.zeros_like(inner)
    acc_gate[...] = jnp.zeros_like(acc_gate)
    for copy in key_copies:
        copy.wait()

    def project(step, carry):
        blends, opens, keys, accepts = [], [], [], []
        for i in range(GROUPS_IN):
            g = step * GROUPS_IN + i
            cols = group_columns(g, lw)
            normed, delta = normed_and_delta(part(g), flag_ref, first_ref, gain_ref, 1, cols, mean, inv)
            last = pick_row(normed, len_ref[0] - 1)
            shift_ref[:, cols] = jnp.concatenate([last_in_ref[:, cols], last], axis=0).astype(BF16)
            mix = mix_ref[:, cols].astype(F32)
            blends.append((normed + delta * mix[5:6]).astype(BF16))
            opens.append((normed + delta * mix[6:7]).astype(BF16))
            keys.append(key_scr[:, cols])
            accepts.append(accept_ref[cols, :])
        inner[...] += nt_dot(jnp.concatenate(blends, axis=1), jnp.concatenate(keys, axis=1))
        acc_gate[...] += nn_dot(jnp.concatenate(opens, axis=1), jnp.concatenate(accepts, axis=0))
        return carry

    lax.fori_loop(0, groups // GROUPS_IN, project, 0)
    positive = jnp.maximum(inner[...], 0.0)
    hidden[...] = (positive * positive).astype(BF16)
    gate_ref[...] = jax.nn.sigmoid(acc_gate[...])
    for copy in value_copies:
        copy.wait()

    def leave(step, carry):
        block = [step * GROUPS_OUT + i for i in range(GROUPS_OUT)]
        values = jnp.concatenate([value_scr[:, group_columns(g, lw)] for g in block], axis=1)
        out = nn_dot(hidden[...], values).astype(BF16)
        for i, g in enumerate(block):
            terms_ref[g] = out[:, i * lw : (i + 1) * lw]
        return carry

    lax.fori_loop(0, groups // GROUPS_OUT, leave, 0)


def channel_mix(length, flag, last_in, x, first, gains, mixes, accept, pieces):
    groups, rows, lw = x.shape
    units = PIECES * pieces[0].shape[0]
    width = groups * lw
    return pl.pallas_call(
        channel_mix_kernel,
        out_shape=(
            jax.ShapeDtypeStruct((groups, rows, lw), BF16),
            jax.ShapeDtypeStruct((rows, lw), F32),
            jax.ShapeDtypeStruct((2, width), BF16),
        ),
        in_specs=[SM, SM] + [VM] * 6 + [HB] * (PIECES + 1),
        out_specs=(VM, VM, VM),
        scratch_shapes=[
            pltpu.VMEM((units, width), BF16),
            pltpu.VMEM((units, width), BF16),
            pltpu.VMEM((rows, units), F32),
            pltpu.VMEM((rows, lw), F32),
            pltpu.VMEM((rows, units), BF16),
            pltpu.SemaphoreType.DMA((PIECES,)),
            pltpu.SemaphoreType.DMA((PIECES,)),
        ],
        compiler_params=pltpu.CompilerParams(vmem_limit_bytes=VMEM_LIMIT),
        cost_estimate=COST,
        name="channel_mix",
    )(length, flag, last_in, x, first, gains, mixes, accept, *pieces)


def hid_place():
    me = lax.axis_index("hid")
    y, z, c = me // (NZ * NC), me // NC % NZ, me % NC

    def at(yy, zz, cc):
        return {"hid": (yy * NZ + zz) * NC + cc}

    zu, zd = (z + 1) % NZ, (z + 3) % NZ
    peers = {"core": at(y, z, 1 - c), "up": at(y, zu, c), "down": at(y, zd, c), "y": at(1 - y, z, c)}
    return y, z, c, zu, (z + 2) % NZ, zd, peers


def meet(peers):
    barrier = pltpu.get_barrier_semaphore()
    for device in peers.values():
        pl.semaphore_signal(barrier, inc=1, device_id=device, device_id_type=MESH)
    pl.semaphore_wait(barrier, len(peers))


class Copies:
    def __init__(self, send, recv):
        self.send, self.recv, self.made = send, recv, []

    def start(self, src, dst, device):
        i = len(self.made)
        copy = pltpu.make_async_remote_copy(
            src_ref=src, dst_ref=dst, send_sem=self.send.at[i], recv_sem=self.recv.at[i],
            device_id=device, device_id_type=MESH,
        )
        copy.start()
        self.made.append(copy)
        return copy

    def finish(self):
        for copy in self.made:
            copy.wait_send()


def sum_terms(terms, acc, core_buf, pass_a, near_a, y_a, pass_b, near_b, y_b, copies, place):
    y, z, c, zu, z2, zd, peers = place
    quarter = terms.shape[3] // 4
    a, a0, a1 = slice(0, 2 * quarter), slice(0, quarter), slice(quarter, 2 * quarter)
    b, b0, b1 = (slice(p.start + 2 * quarter, p.stop + 2 * quarter) for p in (a, a0, a1))
    groups = (z2, zu, zd, z)
    from_core = [copies.start(terms.at[1 - c, g], core_buf.at[g], peers["core"]) for g in groups]

    def add(index, values):
        acc[index] = (acc[index].astype(F32) + values.astype(F32)).astype(BF16)

    def add_core(i):
        g = groups[i]
        from_core[i].wait_recv()
        acc[g] = (terms[c, g].astype(F32) + core_buf[g].astype(F32)).astype(BF16)
        return copies.start(acc.at[g, 1 - y, b], y_b.at[g], peers["y"])

    across_b = [add_core(0)]
    pass_up = copies.start(acc.at[z2, :, a0], pass_a.at[0], peers["up"])
    pass_down = copies.start(acc.at[z2, :, a1], pass_a.at[1], peers["down"])
    across_b += [add_core(1), add_core(2)]
    pass_up.wait_recv()
    add((zu, slice(None), a0), pass_a[0])
    near_up = copies.start(acc.at[zu, :, a], near_a.at[0], peers["up"])
    pass_down.wait_recv()
    add((zd, slice(None), a1), pass_a[1])
    near_down = copies.start(acc.at[zd, :, a], near_a.at[1], peers["down"])
    across_b.append(add_core(3))
    across_b[0].wait_recv()
    add((z2, y, b), y_b[z2])
    pass_b_up = copies.start(acc.at[z2, y, b0], pass_b.at[0], peers["up"])
    pass_b_down = copies.start(acc.at[z2, y, b1], pass_b.at[1], peers["down"])
    across_b[1].wait_recv()
    add((zu, y, b), y_b[zu])
    across_b[2].wait_recv()
    add((zd, y, b), y_b[zd])
    near_up.wait_recv()
    near_down.wait_recv()

    def total_a(yy):
        return acc[z, yy, a].astype(F32) + near_a[0, yy].astype(F32) + near_a[1, yy].astype(F32)

    acc[z, 1 - y, a] = total_a(1 - y).astype(BF16)
    across_a = copies.start(acc.at[z, 1 - y, a], y_a, peers["y"])
    pass_b_up.wait_recv()
    add((zu, y, b0), pass_b[0])
    near_b_up = copies.start(acc.at[zu, y, b], near_b.at[0], peers["up"])
    pass_b_down.wait_recv()
    add((zd, y, b1), pass_b[1])
    near_b_down = copies.start(acc.at[zd, y, b], near_b.at[1], peers["down"])
    across_a.wait_recv()
    upper = total_a(y) + y_a[...].astype(F32)
    across_b[3].wait_recv()
    lower = acc[z, y, b].astype(F32) + y_b[z].astype(F32)
    near_b_up.wait_recv()
    near_b_down.wait_recv()
    lower = lower + near_b[0].astype(F32) + near_b[1].astype(F32)
    return (a, upper), (b, lower)


SUM_COPIES, COLLECT_COPIES = 17, 19


def sum_scratch(shape, copies):
    nc, nz, ny, rows, lw = shape
    half, quarter = rows // 2, rows // 4
    return [
        pltpu.VMEM((nz, ny, rows, lw), BF16),
        pltpu.VMEM((nz, ny, rows, lw), BF16),
        pltpu.VMEM((2, ny, quarter, lw), BF16),
        pltpu.VMEM((2, ny, half, lw), BF16),
        pltpu.VMEM((half, lw), BF16),
        pltpu.VMEM((2, quarter, lw), BF16),
        pltpu.VMEM((2, half, lw), BF16),
        pltpu.VMEM((nz, half, lw), BF16),
        pltpu.SemaphoreType.DMA((copies,)),
        pltpu.SemaphoreType.DMA((copies,)),
    ]


def spread_kernel(
    owner_ref, flag_ref, rec_ref, key_ref, val_ref, kept_ref, entry_ref, exit_ref,
    w_ref, s0_ref, mate_ff, before_ff, after_ff,
    own, got, own_state, got_state, local_sem, sems, state_sems, send_w, recv_w,
):
    me, at = lax.axis_index("hid"), lax.axis_index("req")
    x, w = at // NW, at % NW
    hid, _, lw = own.shape
    block_rows = rec_ref.shape[0]
    heads = lw // HEAD
    peers = {
        "mate": {"req": x * NW + 1 - w},
        "up": {"req": (x + 1) % NX * NW + w},
        "down": {"req": (x + NX - 1) % NX * NW + w},
    }
    barrier = pltpu.get_barrier_semaphore()
    for i in range(1, hid):
        pl.semaphore_signal(
            barrier, inc=1, device_id={"hid": (me + i) % hid}, device_id_type=MESH
        )
    for device in peers.values():
        pl.semaphore_signal(barrier, inc=1, device_id=device, device_id_type=MESH)

    def fill(h):
        cols = pl.ds(pl.multiple_of(h * lw, lw), lw)
        for m, ref in enumerate((rec_ref, key_ref, val_ref)):
            own[h, m * block_rows : (m + 1) * block_rows, :] = ref[:, cols].astype(BF16)

    def fill_state(h):
        state = jnp.concatenate([kept_ref[h * heads + i] for i in range(heads)], axis=1)
        own_state[h] = state.astype(BF16)

    def swap(i, src, dst, sems):
        to = (me + i) % hid
        return pltpu.make_async_remote_copy(
            src_ref=src.at[to], dst_ref=dst.at[me], send_sem=sems.at[0, i - 1],
            recv_sem=sems.at[1, i - 1], device_id={"hid": to}, device_id_type=MESH,
        )

    def fill_and_send(i, carry):
        fill((me + i) % hid)
        swap(i, own, got, sems).start()
        return carry

    def fill_and_send_state(i, carry):
        fill_state((me + i) % hid)
        swap(i, own_state, got_state, state_sems).start()
        return carry

    def arrive(i, carry):
        swap(i, own, got, sems).wait_recv()
        return carry

    def finish(i, carry):
        swap(i, own, got, sems).wait_send()
        swap(i, own_state, got_state, state_sems).wait()
        return carry

    pl.semaphore_wait(barrier, hid - 1 + len(peers))
    copies = Copies(send_w, recv_w)
    units = entry_ref.shape[0]
    halves = [(src, pl.ds(i * units, units)) for i, src in enumerate((entry_ref, exit_ref))]
    first_hops = [copies.start(src, before_ff.at[half], peers["up"]) for src, half in halves]
    first_hops += [copies.start(src, after_ff.at[half], peers["down"]) for src, half in halves]
    lax.fori_loop(1, hid, fill_and_send, 0)
    first_hops += [copies.start(src, mate_ff.at[half], peers["mate"]) for src, half in halves]
    fill(me)
    got[me] = own[me]
    lax.fori_loop(1, hid, arrive, 0)
    mate = x * NW + 1 - w
    before, after = (x + NX - 1) % NX * NW, (x + 1) % NX * NW
    a, b = slice(0, SPLIT), slice(SPLIT, hid)
    b0, b1 = slice(SPLIT, (SPLIT + hid) // 2), slice((SPLIT + hid) // 2, hid)
    keep = pltpu.make_async_copy(got, w_ref.at[at], local_sem)

    def pass_on(index, rows, device, first=False):
        here = w_ref.at[index, rows]
        return copies.start(got.at[rows] if first else here, here, peers[device])

    a_up, a_down = pass_on(at, a, "up", True), pass_on(at, a, "down", True)
    a_mate = pass_on(at, a, "mate", True)
    b_up, b_down = pass_on(at, b, "up", True), pass_on(at, b, "down", True)
    b_mates = [pass_on(at, b, "mate", True)]
    keep.start()
    fill_state(me)
    got_state[me] = own_state[me]
    lax.fori_loop(1, hid, fill_and_send_state, 0)
    a_up.wait_recv()
    far_up = pass_on(before + w, a, "up")
    a_mate.wait_recv()
    mate_up, mate_down = pass_on(mate, a, "up"), pass_on(mate, a, "down")
    a_down.wait_recv()
    b_up.wait_recv()
    b_mates.append(pass_on(before + w, b, "mate"))
    far_b_up = pass_on(before + w, b0, "up")
    b_down.wait_recv()
    far_b_down = pass_on(after + w, b1, "down")
    b_mates.append(pass_on(after + w, b, "mate"))
    mate_down.wait_recv()
    far_down = pass_on(after + 1 - w, a, "down")
    far_b_up.wait_recv()
    far_b_down.wait_recv()
    b_mates.append(pass_on((x + 2) % NX * NW + w, b, "mate"))
    lax.fori_loop(1, hid, finish, 0)
    s0_ref[...] = jnp.where(flag_ref[0] == 1, got_state[owner_ref[0]].astype(F32), 0.0)
    for copy in [mate_up, far_up, far_down] + b_mates + first_hops:
        copy.wait_recv()
    keep.wait()
    copies.finish()


def spread(owner, flag, rec, key, val, kept, entry, exit_rows, hid):
    units = entry.shape[0]
    pair = jax.ShapeDtypeStruct((2 * units, entry.shape[1]), BF16)
    block_rows, width = rec.shape
    lw = width // hid
    req = NX * NW
    return pl.pallas_call(
        spread_kernel,
        out_shape=(
            jax.ShapeDtypeStruct((req, hid, 3 * block_rows, lw), BF16),
            jax.ShapeDtypeStruct((HEAD, lw), F32),
            pair,
            pair,
            pair,
        ),
        in_specs=[SM, SM, VM, VM, VM, VM, HB, HB],
        out_specs=(HB, VM, HB, HB, HB),
        scratch_shapes=[
            pltpu.VMEM((hid, 3 * block_rows, lw), BF16),
            pltpu.VMEM((hid, 3 * block_rows, lw), BF16),
            pltpu.VMEM((hid, HEAD, lw), BF16),
            pltpu.VMEM((hid, HEAD, lw), BF16),
            pltpu.SemaphoreType.DMA,
            pltpu.SemaphoreType.DMA((2, hid - 1)),
            pltpu.SemaphoreType.DMA((2, hid - 1)),
            pltpu.SemaphoreType.DMA((21,)),
            pltpu.SemaphoreType.DMA((21,)),
        ],
        compiler_params=pltpu.CompilerParams(
            collective_id=2, has_side_effects=True, vmem_limit_bytes=VMEM_LIMIT
        ),
        cost_estimate=COST,
        name="spread",
    )(owner, flag, rec, key, val, kept, entry, exit_rows)


def join_kernel(
    terms, x_ref, before_ff, after_mate_ff, mid_ref, own_ref, far_ff, far_mate_ff, *scratch
):
    place = hid_place()
    y, z, c, zu, z2, zd, peers = place
    x, w = lax.axis_index("req") // NW, lax.axis_index("req") % NW
    along_x = {
        "x up": {"req": (x + 1) % NX * NW + w},
        "x down": {"req": (x + NX - 1) % NX * NW + w},
    }
    meet({**peers, **along_x})
    copies = Copies(*scratch[-2:])
    last_hops = [
        copies.start(before_ff, far_ff, along_x["x up"]),
        copies.start(after_mate_ff, far_mate_ff, along_x["x down"]),
    ]
    quarter = x_ref.shape[0] // 4
    every = slice(None)
    a, a0, a1 = slice(0, 2 * quarter), slice(0, quarter), slice(quarter, 2 * quarter)
    b, b0, b1 = (slice(p.start + 2 * quarter, p.stop + 2 * quarter) for p in (a, a0, a1))
    for rows, total in sum_terms(terms, *scratch[:-2], copies, place):
        own = (x_ref[rows].astype(F32) + total).astype(BF16)
        own_ref[rows] = own
        mid_ref[c, z, y, rows] = own

    def pass_on(device, *index):
        return copies.start(mid_ref.at[index], mid_ref.at[index], peers[device])

    across_a = pass_on("y", c, z, y, a)
    near_b_up = pass_on("up", c, z, y, b)
    near_b_down = pass_on("down", c, z, y, b)
    across_b = [pass_on("y", c, z, y, b)]
    across_a.wait_recv()
    near_a_up = pass_on("up", c, z, every, a)
    near_a_down = pass_on("down", c, z, every, a)
    near_b_up.wait_recv()
    far_b_up = pass_on("up", c, zd, y, b0)
    across_b.append(pass_on("y", c, zd, y, b))
    near_b_down.wait_recv()
    far_b_down = pass_on("down", c, zu, y, b1)
    across_b.append(pass_on("y", c, zu, y, b))
    near_a_up.wait_recv()
    far_a_up = pass_on("up", c, zd, every, a0)
    near_a_down.wait_recv()
    far_a_down = pass_on("down", c, zu, every, a1)
    far_b_up.wait_recv()
    far_b_down.wait_recv()
    across_b.append(pass_on("y", c, z2, y, b))
    to_core = []
    for i, g in enumerate((z, zd, zu)):
        across_b[i].wait_recv()
        to_core.append(pass_on("core", c, g))
    far_a_up.wait_recv()
    far_a_down.wait_recv()
    across_b[3].wait_recv()
    to_core.append(pass_on("core", c, z2))
    for copy in to_core + last_hops:
        copy.wait_recv()
    copies.finish()


def join(terms, x_share, before, after_mate):
    rows, lw = x_share.shape
    shape = (NC, NZ, NY, rows, lw)
    return pl.pallas_call(
        join_kernel,
        out_shape=(
            jax.ShapeDtypeStruct(shape, BF16),
            jax.ShapeDtypeStruct((rows, lw), BF16),
            jax.ShapeDtypeStruct(before.shape, BF16),
            jax.ShapeDtypeStruct(before.shape, BF16),
        ),
        in_specs=[VM, VM, HB, HB],
        out_specs=(VM, VM, HB, HB),
        scratch_shapes=sum_scratch(shape, SUM_COPIES + COLLECT_COPIES),
        compiler_params=pltpu.CompilerParams(
            collective_id=0, has_side_effects=True, vmem_limit_bytes=VMEM_LIMIT
        ),
        cost_estimate=COST,
        name="join",
    )(terms.reshape(shape), x_share, before, after_mate)


def close_kernel(len_ref, terms, own_ref, gate_ref, out_ref, *scratch):
    place = hid_place()
    meet(place[-1])
    copies = Copies(*scratch[-2:])
    for rows, total in sum_terms(terms, *scratch[:-2], copies, place):
        combined = own_ref[rows].astype(F32) + gate_ref[rows] * total
        row = lax.broadcasted_iota(jnp.int32, combined.shape, 0) + rows.start
        out_ref[rows] = jnp.where(row < len_ref[0], combined, 0.0).astype(BF16)
    copies.finish()


def close(length, terms, own, gate_rows):
    rows, lw = own.shape
    shape = (NC, NZ, NY, rows, lw)
    return pl.pallas_call(
        close_kernel,
        out_shape=jax.ShapeDtypeStruct((rows, lw), BF16),
        in_specs=[SM, VM, VM, VM],
        out_specs=VM,
        scratch_shapes=sum_scratch(shape, SUM_COPIES),
        compiler_params=pltpu.CompilerParams(
            collective_id=1, has_side_effects=True, vmem_limit_bytes=VMEM_LIMIT
        ),
        name="close",
    )(length, terms.reshape(shape), own, gate_rows)


def local(
    input_activations,
    prompt_extents,
    continuing_flags,
    owning_index,
    partition_arrangement,
    training_accept_pieces,
    training_lookup_pieces,
    training_content_pieces,
    normalizer_scales,
    prior_step_blends,
    forgetting_bias_vector,
    forgetting_left_lowrank,
    forgetting_right_lowrank,
    instant_emphasis,
    group_normalizer_scale,
    gating_projection,
    mixing_exit_projection,
    kept_summary_places,
    previous_normed_entries,
    feedforward_entry_proj,
    feedforward_exit_proj,
    feedforward_accept_proj,
):
    x = input_activations[0]
    rows, width = x.shape
    lw = mixing_exit_projection.shape[0]
    hid = lax.axis_size("hid")
    block_rows = training_accept_pieces.shape[0]
    w, s0, mate, before, after = spread(
        owning_index, continuing_flags, training_accept_pieces, training_lookup_pieces,
        training_content_pieces, kept_summary_places[0, 0], feedforward_entry_proj,
        feedforward_exit_proj, hid,
    )
    before_mate, after_mate = send(mate, 1, 0), send(mate, NX - 1, 0)
    w = w.reshape(-1, 3 * block_rows, lw)
    terms, state, last_in, x_share = time_mix(
        partition_arrangement, prompt_extents, continuing_flags, x, previous_normed_entries[0],
        normalizer_scales, prior_step_blends,
        gating_projection, forgetting_left_lowrank, forgetting_right_lowrank,
        forgetting_bias_vector[None], instant_emphasis[None], group_normalizer_scale[None],
        s0, mixing_exit_projection, w,
    )
    middle, own_middle, far, far_mate = join(terms, x_share, before, after_mate)
    out_terms, gate_rows, shift_out = channel_mix(
        prompt_extents, continuing_flags, last_in, middle.reshape(hid, rows, lw),
        previous_normed_entries[0], normalizer_scales, prior_step_blends, feedforward_accept_proj,
        [feedforward_entry_proj, feedforward_exit_proj, mate, before, after, before_mate, after_mate, far, far_mate],
    )
    layer_out = close(prompt_extents, out_terms, own_middle, gate_rows)[None]
    return (layer_out, state[None], shift_out[None])


def solution(mesh):
    placed = (
        P("req", None, None),
        P("req"),
        P("req"),
        P("req"),
        P(),
        P(("req", "hid"), None),
        P(("req", "hid"), None),
        P(("req", "hid"), None),
        P(),
        P(),
        P("hid"),
        P(),
        P(None, "hid"),
        P("hid"),
        P("hid"),
        P(None, "hid"),
        P("hid", None),
        P("req", "hid", None, None, None),
        P("req", None, None),
        P(("req", "hid"), None),
        P(("req", "hid"), None),
        P(None, "hid"),
    )
    return jax.shard_map(
        local,
        mesh=mesh,
        in_specs=placed,
        out_specs=(P("req", None, "hid"), P("req", "hid", None, None), P("req", None, None)),
        check_vma=False,
    )
```

```python
from functools import partial

import jax
import jax.numpy as jnp
from jax import lax
from jax.experimental import pallas as pl
from jax.experimental.pallas import tpu as pltpu
from jax.sharding import PartitionSpec as P

HEAD = 64
CHUNK = 16
TILE = 64
PAIR = 128
KC = 512
GROUPS_IN, GROUPS_OUT = 4, 4
VMEM_LIMIT = 58 * 1024 * 1024
F32 = jnp.float32
BF16 = jnp.bfloat16
MESH = pl.DeviceIdType.MESH
NY, NZ, NC = 2, 4, 2
NX, NW = 4, 2
PIECES = NX * NW
ROW_REFS = 1 + NX + 2 * NX
REST = 32
SPLIT = 9
COST = pl.CostEstimate(flops=40_000_000_000, bytes_accessed=40_000_000, transcendentals=0)
VM = pl.BlockSpec(memory_space=pltpu.VMEM)
SM = pl.BlockSpec(memory_space=pltpu.SMEM)
HB = pl.BlockSpec(memory_space=pl.ANY)


def nt_dot(a, b):
    return lax.dot_general(a, b, (((1,), (1,)), ((), ())), preferred_element_type=F32)


def tn_dot(a, b):
    return lax.dot_general(a, b, (((0,), (0,)), ((), ())), preferred_element_type=F32)


def nn_dot(a, b):
    return jnp.dot(a, b, preferred_element_type=F32)


def send(value, dx, dw):
    pairs = [(x * NW + w, (x + dx) % NX * NW + (w + dw) % NW) for x in range(NX) for w in range(NW)]
    return lax.ppermute(value, "req", pairs)


def group_columns(g, lw):
    block = (g % NY) * (NZ * NC) + (g // NY % NZ) * NC + g // (NY * NZ)
    return pl.ds(pl.multiple_of(block * lw, lw), lw)


def row_stats(part, count, rows, width, eps):
    def add_sum(c, total):
        return total + jnp.sum(part(c), axis=1, keepdims=True)

    def add_square(c, total):
        center = part(c) - mean
        return total + jnp.sum(center * center, axis=1, keepdims=True)

    zero = jnp.zeros((rows, 1), F32)
    mean = lax.fori_loop(0, count, add_sum, zero) / width
    var = lax.fori_loop(0, count, add_square, zero) / width
    return mean, 1.0 / jnp.sqrt(var + eps)


def normed_and_delta(part, flag_ref, first_ref, gain_ref, which, cols, mean, inv):
    normed = (part - mean) * inv * gain_ref[:, cols].astype(F32)[which : which + 1]
    before = pltpu.roll(normed, 1, 0)
    row = lax.broadcasted_iota(jnp.int32, normed.shape, 0)
    saved = first_ref[:, cols].astype(F32)[which : which + 1]
    before = jnp.where(row == 0, jnp.where(flag_ref[0] == 1, saved, 0.0), before)
    return normed, before - normed


def pick_row(values, index):
    row = lax.broadcasted_iota(jnp.int32, values.shape, 0)
    return jnp.sum(jnp.where(row == index, values, 0.0), axis=0, keepdims=True)


def time_mix_kernel(
    perm_ref, len_ref, flag_ref, x_ref, first_ref, gain_ref, mix_ref, gating_ref, left_ref,
    right_ref, bias_ref, bonus_ref, gscale_ref, s0_ref, exit_ref, w_ref,
    terms_ref, state_ref, last_ref, share_ref,
    w_scr, acc, acc_low, acc_gate, logw_scr, prod_scr, gated_scr, st_scr, sem,
):
    rows, width = x_ref.shape
    block_rows = w_scr.shape[1] // 3
    lw = acc_gate.shape[1]


    def start(j, carry):
        pltpu.make_async_copy(w_ref.at[j], w_scr.at[perm_ref[j]], sem).start()
        return carry

    lax.fori_loop(0, w_scr.shape[0], start, 0)
    share_ref[...] = x_ref[:, pl.ds(pl.multiple_of(lax.axis_index("hid") * lw, lw), lw)]

    def part(c):
        return x_ref[:, pl.ds(pl.multiple_of(c * KC, KC), KC)].astype(F32)

    mean, inv = row_stats(part, width // KC, rows, width, 1e-05)
    acc[...] = jnp.zeros_like(acc)
    acc_low[...] = jnp.zeros_like(acc_low)
    acc_gate[...] = jnp.zeros_like(acc_gate)
    pltpu.make_async_copy(w_scr, w_scr, sem).wait()
    per = KC // block_rows

    def project(c, carry):
        cols = pl.ds(pl.multiple_of(c * KC, KC), KC)
        normed, delta = normed_and_delta(part(c), flag_ref, first_ref, gain_ref, 0, cols, mean, inv)
        last_ref[:, cols] = pick_row(normed, len_ref[0] - 1)
        mix = mix_ref[:, cols].astype(F32)

        def blend(m):
            return (normed + delta * mix[m : m + 1]).astype(BF16)

        for m in range(3):
            own_rows = slice(m * block_rows, (m + 1) * block_rows)
            wm = w_scr[pl.ds(c * per, per), own_rows, :].reshape(KC, lw)
            acc[:, m * lw : (m + 1) * lw] += nn_dot(blend(m), wm)
        acc_low[...] += nn_dot(blend(3), left_ref[cols, :])
        acc_gate[...] += nn_dot(blend(4), gating_ref[cols, :])
        return carry

    lax.fori_loop(0, width // KC, project, 0)
    length = len_ref[0]
    present = lax.broadcasted_iota(jnp.int32, (rows, lw), 0) < length
    low = jnp.tanh(acc_low[...]).astype(BF16)
    log_decay = -jnp.exp(bias_ref[...] + nn_dot(low, right_ref[...]))
    logw_scr[...] = jnp.where(present, log_decay, 0.0)
    acc[:, lw : 2 * lw] = jnp.where(present, acc[:, lw : 2 * lw], 0.0)

    pairs = lw // PAIR

    def same_head(size):
        a = lax.broadcasted_iota(jnp.int32, (size, size), 0) // HEAD
        b = lax.broadcasted_iota(jnp.int32, (size, size), 1) // HEAD
        return a == b

    pair_mask = same_head(PAIR)
    for p in range(pairs):
        two = s0_ref[:, p * PAIR : (p + 1) * PAIR]
        st_scr[p] = jnp.where(pair_mask, jnp.concatenate([two, two], axis=0), 0.0).T

    ones = jnp.where(same_head(lw), 1.0, 0.0).astype(BF16)
    slot = lax.broadcasted_iota(jnp.int32, (TILE, lw), 0) % CHUNK

    def head_sum(values):
        high = values.astype(BF16)
        rest = (values - high.astype(F32)).astype(BF16)
        return nn_dot(high, ones) + nn_dot(rest, ones)

    def tile_step(t, carry):
        here = pl.ds(pl.multiple_of(t * TILE, TILE), TILE)
        r = acc[here, 0:lw]
        k = acc[here, lw : 2 * lw]
        v = acc[here, 2 * lw : 3 * lw]
        decay = logw_scr[here, :]
        incl = decay
        step = 1
        while step < CHUNK:
            incl = incl + jnp.where(slot >= step, pltpu.roll(incl, step, 0), 0.0)
            step *= 2
        excl = incl - decay
        prod_scr[0:TILE, :] = (r * bonus_ref[...] * k).astype(BF16)
        for d in range(1, CHUNK):
            gap = jnp.minimum(excl - pltpu.roll(incl, d, 0), 0.0)
            term = jnp.where(slot >= d, r * pltpu.roll(k, d, 0) * jnp.exp(gap), 0.0)
            prod_scr[d * TILE : (d + 1) * TILE, :] = term.astype(BF16)
        scores = nn_dot(prod_scr[...], ones)
        out = scores[0:TILE] * v
        for d in range(1, CHUNK):
            out = out + scores[d * TILE : (d + 1) * TILE] * pltpu.roll(v, d, 0)
        rw = (r * jnp.exp(excl)).astype(BF16)
        vb = v.astype(BF16)
        pieces = []
        for c in range(TILE // CHUNK):
            lo, hi = c * CHUNK, (c + 1) * CHUNK
            closing = incl[hi - 1 : hi]
            kw = (k[lo:hi] * jnp.exp(closing - incl[lo:hi])).astype(BF16)
            fade = jnp.exp(closing)
            parts = []
            for p in range(pairs):
                a, b = p * PAIR, (p + 1) * PAIR
                st = st_scr[p]
                parts.append(nt_dot(rw[lo:hi, a:b], st.astype(BF16)))
                grown = tn_dot(vb[lo:hi, a:b], kw[:, a:b])
                st_scr[p] = st * fade[:, a:b] + jnp.where(pair_mask, grown, 0.0)
            pieces.append(jnp.concatenate(parts, axis=1))
        out = out + jnp.concatenate(pieces, axis=0)
        center = out - head_sum(out) * (1.0 / HEAD)
        spread = head_sum(center * center) * (1.0 / HEAD)
        grouped = center / jnp.sqrt(spread + 0.00064) * gscale_ref[...]
        g = acc_gate[here, :]
        gate = g / (1.0 + jnp.exp(-g))
        gated_scr[here, :] = (grouped * gate).astype(BF16)
        return carry

    lax.fori_loop(0, rows // TILE, tile_step, 0)
    for p in range(pairs):
        full = st_scr[p].T
        state_ref[2 * p] = full[0:HEAD, 0:HEAD]
        state_ref[2 * p + 1] = full[HEAD:PAIR, HEAD:PAIR]

    def leave(g, carry):
        terms_ref[g] = nn_dot(gated_scr[...], exit_ref[:, group_columns(g, lw)]).astype(BF16)
        return carry

    lax.fori_loop(0, width // lw, leave, 0)


def time_mix(perm, length, flag, x, first, gains, mixes, gating, left, right, bias, bonus, gscale, s0, exit_w, w):
    rows, width = x.shape
    lw = gating.shape[1]
    return pl.pallas_call(
        time_mix_kernel,
        out_shape=(
            jax.ShapeDtypeStruct((width // lw, rows, lw), BF16),
            jax.ShapeDtypeStruct((lw // HEAD, HEAD, HEAD), F32),
            jax.ShapeDtypeStruct((1, width), F32),
            jax.ShapeDtypeStruct((rows, lw), BF16),
        ),
        in_specs=[SM, SM, SM] + [VM] * 12 + [HB],
        out_specs=(VM, VM, VM, VM),
        scratch_shapes=[
            pltpu.VMEM(w.shape, BF16),
            pltpu.VMEM((rows, 3 * lw), F32),
            pltpu.VMEM((rows, left.shape[1]), F32),
            pltpu.VMEM((rows, lw), F32),
            pltpu.VMEM((rows, lw), F32),
            pltpu.VMEM((CHUNK * TILE, lw), BF16),
            pltpu.VMEM((rows, lw), BF16),
            pltpu.VMEM((lw // PAIR, PAIR, PAIR), F32),
            pltpu.SemaphoreType.DMA,
        ],
        compiler_params=pltpu.CompilerParams(vmem_limit_bytes=VMEM_LIMIT),
        cost_estimate=COST,
        name="time_mix",
    )(perm, length, flag, x, first, gains, mixes, gating, left, right, bias, bonus, gscale, s0, exit_w, w)


def channel_mix_kernel(
    len_ref, flag_ref, last_in_ref, x_ref, first_ref, gain_ref, mix_ref, accept_ref, *refs,
):
    entry_ref, exit_ref = refs[:2]
    whole, cut, rests = refs[2:NX + 1], refs[NX + 1 : 2 * NX + 1], refs[2 * NX + 1 : ROW_REFS]
    terms_ref, gate_ref, shift_ref = refs[ROW_REFS : ROW_REFS + 3]
    key_scr, value_scr, inner, acc_gate, hidden, key_sems, value_sems = refs[ROW_REFS + 3 :]
    groups, rows, lw = x_ref.shape
    units = entry_ref.shape[0]

    def fetch(pieces, scr, sems):
        copies, begin = [], 0
        for i, piece in enumerate(pieces):
            count = piece.shape[0]
            copies.append(
                pltpu.make_async_copy(piece, scr.at[pl.ds(begin, count)], sems.at[i])
            )
            begin += count
        for copy in copies:
            copy.start()
        return copies

    keys = [entry_ref] + [piece.at[pl.ds(0, units)] for piece in whole + cut]
    values = [exit_ref] + [piece.at[pl.ds(units, units)] for piece in whole]
    for piece, rest in zip(cut, rests):
        values += [piece.at[pl.ds(units, units - REST)], rest]
    key_copies = fetch(keys, key_scr, key_sems)
    value_copies = fetch(values, value_scr, value_sems)

    def part(g):
        return x_ref[g].astype(F32)

    mean, inv = row_stats(part, groups, rows, groups * lw, 1e-05)
    inner[...] = jnp.zeros_like(inner)
    acc_gate[...] = jnp.zeros_like(acc_gate)
    for copy in key_copies:
        copy.wait()

    def project(step, carry):
        blends, opens, keys, accepts = [], [], [], []
        for i in range(GROUPS_IN):
            g = step * GROUPS_IN + i
            cols = group_columns(g, lw)
            normed, delta = normed_and_delta(part(g), flag_ref, first_ref, gain_ref, 1, cols, mean, inv)
            last = pick_row(normed, len_ref[0] - 1)
            shift_ref[:, cols] = jnp.concatenate([last_in_ref[:, cols], last], axis=0).astype(BF16)
            mix = mix_ref[:, cols].astype(F32)
            blends.append((normed + delta * mix[5:6]).astype(BF16))
            opens.append((normed + delta * mix[6:7]).astype(BF16))
            keys.append(key_scr[:, cols])
            accepts.append(accept_ref[cols, :])
        inner[...] += nt_dot(jnp.concatenate(blends, axis=1), jnp.concatenate(keys, axis=1))
        acc_gate[...] += nn_dot(jnp.concatenate(opens, axis=1), jnp.concatenate(accepts, axis=0))
        return carry

    lax.fori_loop(0, groups // GROUPS_IN, project, 0)
    positive = jnp.maximum(inner[...], 0.0)
    hidden[...] = (positive * positive).astype(BF16)
    gate_ref[...] = jax.nn.sigmoid(acc_gate[...])
    for copy in value_copies:
        copy.wait()

    def leave(step, carry):
        block = [step * GROUPS_OUT + i for i in range(GROUPS_OUT)]
        values = jnp.concatenate([value_scr[:, group_columns(g, lw)] for g in block], axis=1)
        out = nn_dot(hidden[...], values).astype(BF16)
        for i, g in enumerate(block):
            terms_ref[g] = out[:, i * lw : (i + 1) * lw]
        return carry

    lax.fori_loop(0, groups // GROUPS_OUT, leave, 0)


def channel_mix(length, flag, last_in, x, first, gains, mixes, accept, pieces):
    groups, rows, lw = x.shape
    units = PIECES * pieces[0].shape[0]
    width = groups * lw
    return pl.pallas_call(
        channel_mix_kernel,
        out_shape=(
            jax.ShapeDtypeStruct((groups, rows, lw), BF16),
            jax.ShapeDtypeStruct((rows, lw), F32),
            jax.ShapeDtypeStruct((2, width), BF16),
        ),
        in_specs=[SM, SM] + [VM] * 6 + [HB] * ROW_REFS,
        out_specs=(VM, VM, VM),
        scratch_shapes=[
            pltpu.VMEM((units, width), BF16),
            pltpu.VMEM((units, width), BF16),
            pltpu.VMEM((rows, units), F32),
            pltpu.VMEM((rows, lw), F32),
            pltpu.VMEM((rows, units), BF16),
            pltpu.SemaphoreType.DMA((PIECES,)),
            pltpu.SemaphoreType.DMA((PIECES + NX,)),
        ],
        compiler_params=pltpu.CompilerParams(vmem_limit_bytes=VMEM_LIMIT),
        cost_estimate=COST,
        name="channel_mix",
    )(length, flag, last_in, x, first, gains, mixes, accept, *pieces)


def hid_place():
    me = lax.axis_index("hid")
    y, z, c = me // (NZ * NC), me // NC % NZ, me % NC

    def at(yy, zz, cc):
        return {"hid": (yy * NZ + zz) * NC + cc}

    zu, zd = (z + 1) % NZ, (z + 3) % NZ
    peers = {"core": at(y, z, 1 - c), "up": at(y, zu, c), "down": at(y, zd, c), "y": at(1 - y, z, c)}
    return y, z, c, zu, (z + 2) % NZ, zd, peers


def meet(peers):
    barrier = pltpu.get_barrier_semaphore()
    for device in peers.values():
        pl.semaphore_signal(barrier, inc=1, device_id=device, device_id_type=MESH)
    pl.semaphore_wait(barrier, len(peers))


class Copies:
    def __init__(self, send, recv):
        self.send, self.recv, self.made = send, recv, []

    def start(self, src, dst, device):
        i = len(self.made)
        copy = pltpu.make_async_remote_copy(
            src_ref=src, dst_ref=dst, send_sem=self.send.at[i], recv_sem=self.recv.at[i],
            device_id=device, device_id_type=MESH,
        )
        copy.start()
        self.made.append(copy)
        return copy

    def finish(self):
        for copy in self.made:
            copy.wait_send()


def sum_terms(terms, acc, core_buf, pass_a, near_a, y_a, pass_b, near_b, y_b, copies, place):
    y, z, c, zu, z2, zd, peers = place
    quarter = terms.shape[3] // 4
    a, a0, a1 = slice(0, 2 * quarter), slice(0, quarter), slice(quarter, 2 * quarter)
    b, b0, b1 = (slice(p.start + 2 * quarter, p.stop + 2 * quarter) for p in (a, a0, a1))
    groups = (z2, zu, zd, z)
    from_core = [copies.start(terms.at[1 - c, g], core_buf.at[g], peers["core"]) for g in groups]

    def add(index, values):
        acc[index] = (acc[index].astype(F32) + values.astype(F32)).astype(BF16)

    def add_core(i):
        g = groups[i]
        from_core[i].wait_recv()
        acc[g] = (terms[c, g].astype(F32) + core_buf[g].astype(F32)).astype(BF16)
        return copies.start(acc.at[g, 1 - y, b], y_b.at[g], peers["y"])

    across_b = [add_core(0)]
    pass_up = copies.start(acc.at[z2, :, a0], pass_a.at[0], peers["up"])
    pass_down = copies.start(acc.at[z2, :, a1], pass_a.at[1], peers["down"])
    across_b += [add_core(1), add_core(2)]
    pass_up.wait_recv()
    add((zu, slice(None), a0), pass_a[0])
    near_up = copies.start(acc.at[zu, :, a], near_a.at[0], peers["up"])
    pass_down.wait_recv()
    add((zd, slice(None), a1), pass_a[1])
    near_down = copies.start(acc.at[zd, :, a], near_a.at[1], peers["down"])
    across_b.append(add_core(3))
    across_b[0].wait_recv()
    add((z2, y, b), y_b[z2])
    pass_b_up = copies.start(acc.at[z2, y, b0], pass_b.at[0], peers["up"])
    pass_b_down = copies.start(acc.at[z2, y, b1], pass_b.at[1], peers["down"])
    across_b[1].wait_recv()
    add((zu, y, b), y_b[zu])
    across_b[2].wait_recv()
    add((zd, y, b), y_b[zd])
    near_up.wait_recv()
    near_down.wait_recv()

    def total_a(yy):
        return acc[z, yy, a].astype(F32) + near_a[0, yy].astype(F32) + near_a[1, yy].astype(F32)

    acc[z, 1 - y, a] = total_a(1 - y).astype(BF16)
    across_a = copies.start(acc.at[z, 1 - y, a], y_a, peers["y"])
    pass_b_up.wait_recv()
    add((zu, y, b0), pass_b[0])
    near_b_up = copies.start(acc.at[zu, y, b], near_b.at[0], peers["up"])
    pass_b_down.wait_recv()
    add((zd, y, b1), pass_b[1])
    near_b_down = copies.start(acc.at[zd, y, b], near_b.at[1], peers["down"])
    across_a.wait_recv()
    upper = total_a(y) + y_a[...].astype(F32)
    across_b[3].wait_recv()
    lower = acc[z, y, b].astype(F32) + y_b[z].astype(F32)
    near_b_up.wait_recv()
    near_b_down.wait_recv()
    lower = lower + near_b[0].astype(F32) + near_b[1].astype(F32)
    return (a, upper), (b, lower)


SUM_COPIES, COLLECT_COPIES = 17, 22


def sum_scratch(shape, copies):
    nc, nz, ny, rows, lw = shape
    half, quarter = rows // 2, rows // 4
    return [
        pltpu.VMEM((nz, ny, rows, lw), BF16),
        pltpu.VMEM((nz, ny, rows, lw), BF16),
        pltpu.VMEM((2, ny, quarter, lw), BF16),
        pltpu.VMEM((2, ny, half, lw), BF16),
        pltpu.VMEM((half, lw), BF16),
        pltpu.VMEM((2, quarter, lw), BF16),
        pltpu.VMEM((2, half, lw), BF16),
        pltpu.VMEM((nz, half, lw), BF16),
        pltpu.SemaphoreType.DMA((copies,)),
        pltpu.SemaphoreType.DMA((copies,)),
    ]


def spread_kernel(
    owner_ref, flag_ref, rec_ref, key_ref, val_ref, kept_ref, entry_ref, exit_ref,
    w_ref, s0_ref, mate_ff, rest_ff, before_ff, after_ff,
    own, got, own_state, got_state, local_sem, sems, state_sems, send_w, recv_w,
):
    me, at = lax.axis_index("hid"), lax.axis_index("req")
    x, w = at // NW, at % NW
    hid, _, lw = own.shape
    block_rows = rec_ref.shape[0]
    heads = lw // HEAD
    peers = {
        "mate": {"req": x * NW + 1 - w},
        "up": {"req": (x + 1) % NX * NW + w},
        "down": {"req": (x + NX - 1) % NX * NW + w},
    }
    barrier = pltpu.get_barrier_semaphore()
    for i in range(1, hid):
        pl.semaphore_signal(
            barrier, inc=1, device_id={"hid": (me + i) % hid}, device_id_type=MESH
        )
    for device in peers.values():
        pl.semaphore_signal(barrier, inc=1, device_id=device, device_id_type=MESH)

    def fill(h):
        cols = pl.ds(pl.multiple_of(h * lw, lw), lw)
        for m, ref in enumerate((rec_ref, key_ref, val_ref)):
            own[h, m * block_rows : (m + 1) * block_rows, :] = ref[:, cols].astype(BF16)

    def fill_state(h):
        state = jnp.concatenate([kept_ref[h * heads + i] for i in range(heads)], axis=1)
        own_state[h] = state.astype(BF16)

    def swap(i, src, dst, sems):
        to = (me + i) % hid
        return pltpu.make_async_remote_copy(
            src_ref=src.at[to], dst_ref=dst.at[me], send_sem=sems.at[0, i - 1],
            recv_sem=sems.at[1, i - 1], device_id={"hid": to}, device_id_type=MESH,
        )

    def fill_and_send(i, carry):
        fill((me + i) % hid)
        swap(i, own, got, sems).start()
        return carry

    def fill_and_send_state(i, carry):
        fill_state((me + i) % hid)
        swap(i, own_state, got_state, state_sems).start()
        return carry

    def arrive(i, carry):
        swap(i, own, got, sems).wait_recv()
        return carry

    def finish(i, carry):
        swap(i, own, got, sems).wait_send()
        swap(i, own_state, got_state, state_sems).wait()
        return carry

    pl.semaphore_wait(barrier, hid - 1 + len(peers))
    copies = Copies(send_w, recv_w)
    units = entry_ref.shape[0]
    halves = [(src, pl.ds(i * units, units)) for i, src in enumerate((entry_ref, exit_ref))]
    first_hops = [copies.start(src, before_ff.at[half], peers["up"]) for src, half in halves]
    first_hops += [copies.start(src, after_ff.at[half], peers["down"]) for src, half in halves]
    lax.fori_loop(1, hid, fill_and_send, 0)
    first_hops += [
        copies.start(entry_ref, mate_ff.at[pl.ds(0, units)], peers["mate"]),
        copies.start(
            exit_ref.at[pl.ds(0, units - REST)], mate_ff.at[pl.ds(units, units - REST)], peers["mate"]
        ),
        copies.start(exit_ref.at[pl.ds(units - REST, REST)], rest_ff, peers["mate"]),
    ]
    fill(me)
    got[me] = own[me]
    lax.fori_loop(1, hid, arrive, 0)
    mate = x * NW + 1 - w
    before, after = (x + NX - 1) % NX * NW, (x + 1) % NX * NW
    a, b = slice(0, SPLIT), slice(SPLIT, hid)
    b0, b1 = slice(SPLIT, (SPLIT + hid) // 2), slice((SPLIT + hid) // 2, hid)
    keep = pltpu.make_async_copy(got, w_ref.at[at], local_sem)

    def pass_on(index, rows, device, first=False):
        here = w_ref.at[index, rows]
        return copies.start(got.at[rows] if first else here, here, peers[device])

    a_up, a_down = pass_on(at, a, "up", True), pass_on(at, a, "down", True)
    a_mate = pass_on(at, a, "mate", True)
    b_up, b_down = pass_on(at, b, "up", True), pass_on(at, b, "down", True)
    b_mates = [pass_on(at, b, "mate", True)]
    keep.start()
    fill_state(me)
    got_state[me] = own_state[me]
    lax.fori_loop(1, hid, fill_and_send_state, 0)
    a_up.wait_recv()
    far_up = pass_on(before + w, a, "up")
    a_mate.wait_recv()
    mate_up, mate_down = pass_on(mate, a, "up"), pass_on(mate, a, "down")
    a_down.wait_recv()
    b_up.wait_recv()
    b_mates.append(pass_on(before + w, b, "mate"))
    far_b_up = pass_on(before + w, b0, "up")
    b_down.wait_recv()
    far_b_down = pass_on(after + w, b1, "down")
    b_mates.append(pass_on(after + w, b, "mate"))
    mate_down.wait_recv()
    far_down = pass_on(after + 1 - w, a, "down")
    far_b_up.wait_recv()
    far_b_down.wait_recv()
    b_mates.append(pass_on((x + 2) % NX * NW + w, b, "mate"))
    lax.fori_loop(1, hid, finish, 0)
    s0_ref[...] = jnp.where(flag_ref[0] == 1, got_state[owner_ref[0]].astype(F32), 0.0)
    for copy in [mate_up, far_up, far_down] + b_mates + first_hops:
        copy.wait_recv()
    keep.wait()
    copies.finish()


def spread(owner, flag, rec, key, val, kept, entry, exit_rows, hid):
    units = entry.shape[0]
    pair = jax.ShapeDtypeStruct((2 * units, entry.shape[1]), BF16)
    block_rows, width = rec.shape
    lw = width // hid
    req = NX * NW
    return pl.pallas_call(
        spread_kernel,
        out_shape=(
            jax.ShapeDtypeStruct((req, hid, 3 * block_rows, lw), BF16),
            jax.ShapeDtypeStruct((HEAD, lw), F32),
            jax.ShapeDtypeStruct((2 * units - REST, entry.shape[1]), BF16),
            jax.ShapeDtypeStruct((REST, entry.shape[1]), BF16),
            pair,
            pair,
        ),
        in_specs=[SM, SM, VM, VM, VM, VM, HB, HB],
        out_specs=(HB, VM, HB, HB, HB, HB),
        scratch_shapes=[
            pltpu.VMEM((hid, 3 * block_rows, lw), BF16),
            pltpu.VMEM((hid, 3 * block_rows, lw), BF16),
            pltpu.VMEM((hid, HEAD, lw), BF16),
            pltpu.VMEM((hid, HEAD, lw), BF16),
            pltpu.SemaphoreType.DMA,
            pltpu.SemaphoreType.DMA((2, hid - 1)),
            pltpu.SemaphoreType.DMA((2, hid - 1)),
            pltpu.SemaphoreType.DMA((22,)),
            pltpu.SemaphoreType.DMA((22,)),
        ],
        compiler_params=pltpu.CompilerParams(
            collective_id=2, has_side_effects=True, vmem_limit_bytes=VMEM_LIMIT
        ),
        cost_estimate=COST,
        name="spread",
    )(owner, flag, rec, key, val, kept, entry, exit_rows)


def join_kernel(
    terms, x_ref, before_ff, after_mate_ff, rest_ff,
    mid_ref, own_ref, far_ff, far_mate_ff, before_rest_ff, after_rest_ff, far_rest_ff, *scratch
):
    place = hid_place()
    y, z, c, zu, z2, zd, peers = place
    x, w = lax.axis_index("req") // NW, lax.axis_index("req") % NW
    along_x = {
        "x up": {"req": (x + 1) % NX * NW + w},
        "x down": {"req": (x + NX - 1) % NX * NW + w},
    }
    meet({**peers, **along_x})
    copies = Copies(*scratch[-2:])
    rest_down = copies.start(rest_ff, after_rest_ff, along_x["x down"])
    last_hops = [
        copies.start(rest_ff, before_rest_ff, along_x["x up"]),
        copies.start(before_ff, far_ff, along_x["x up"]),
        copies.start(after_mate_ff, far_mate_ff, along_x["x down"]),
    ]
    quarter = x_ref.shape[0] // 4
    every = slice(None)
    a, a0, a1 = slice(0, 2 * quarter), slice(0, quarter), slice(quarter, 2 * quarter)
    b, b0, b1 = (slice(p.start + 2 * quarter, p.stop + 2 * quarter) for p in (a, a0, a1))
    for rows, total in sum_terms(terms, *scratch[:-2], copies, place):
        own = (x_ref[rows].astype(F32) + total).astype(BF16)
        own_ref[rows] = own
        mid_ref[c, z, y, rows] = own
    rest_down.wait_recv()
    last_hops.append(copies.start(after_rest_ff, far_rest_ff, along_x["x down"]))

    def pass_on(device, *index):
        return copies.start(mid_ref.at[index], mid_ref.at[index], peers[device])

    across_a = pass_on("y", c, z, y, a)
    near_b_up = pass_on("up", c, z, y, b)
    near_b_down = pass_on("down", c, z, y, b)
    across_b = [pass_on("y", c, z, y, b)]
    across_a.wait_recv()
    near_a_up = pass_on("up", c, z, every, a)
    near_a_down = pass_on("down", c, z, every, a)
    near_b_up.wait_recv()
    far_b_up = pass_on("up", c, zd, y, b0)
    across_b.append(pass_on("y", c, zd, y, b))
    near_b_down.wait_recv()
    far_b_down = pass_on("down", c, zu, y, b1)
    across_b.append(pass_on("y", c, zu, y, b))
    near_a_up.wait_recv()
    far_a_up = pass_on("up", c, zd, every, a0)
    near_a_down.wait_recv()
    far_a_down = pass_on("down", c, zu, every, a1)
    far_b_up.wait_recv()
    far_b_down.wait_recv()
    across_b.append(pass_on("y", c, z2, y, b))
    to_core = []
    for i, g in enumerate((z, zd, zu)):
        across_b[i].wait_recv()
        to_core.append(pass_on("core", c, g))
    far_a_up.wait_recv()
    far_a_down.wait_recv()
    across_b[3].wait_recv()
    to_core.append(pass_on("core", c, z2))
    for copy in to_core + last_hops:
        copy.wait_recv()
    copies.finish()


def join(terms, x_share, before, after_mate, rest):
    rows, lw = x_share.shape
    shape = (NC, NZ, NY, rows, lw)
    return pl.pallas_call(
        join_kernel,
        out_shape=(
            jax.ShapeDtypeStruct(shape, BF16),
            jax.ShapeDtypeStruct((rows, lw), BF16),
            jax.ShapeDtypeStruct(before.shape, BF16),
            jax.ShapeDtypeStruct(after_mate.shape, BF16),
        )
        + (jax.ShapeDtypeStruct(rest.shape, BF16),) * 3,
        in_specs=[VM, VM, HB, HB, HB],
        out_specs=(VM, VM, HB, HB, HB, HB, HB),
        scratch_shapes=sum_scratch(shape, SUM_COPIES + COLLECT_COPIES),
        compiler_params=pltpu.CompilerParams(
            collective_id=0, has_side_effects=True, vmem_limit_bytes=VMEM_LIMIT
        ),
        cost_estimate=COST,
        name="join",
    )(terms.reshape(shape), x_share, before, after_mate, rest)


def close_kernel(len_ref, terms, own_ref, gate_ref, out_ref, *scratch):
    place = hid_place()
    meet(place[-1])
    copies = Copies(*scratch[-2:])
    for rows, total in sum_terms(terms, *scratch[:-2], copies, place):
        combined = own_ref[rows].astype(F32) + gate_ref[rows] * total
        row = lax.broadcasted_iota(jnp.int32, combined.shape, 0) + rows.start
        out_ref[rows] = jnp.where(row < len_ref[0], combined, 0.0).astype(BF16)
    copies.finish()


def close(length, terms, own, gate_rows):
    rows, lw = own.shape
    shape = (NC, NZ, NY, rows, lw)
    return pl.pallas_call(
        close_kernel,
        out_shape=jax.ShapeDtypeStruct((rows, lw), BF16),
        in_specs=[SM, VM, VM, VM],
        out_specs=VM,
        scratch_shapes=sum_scratch(shape, SUM_COPIES),
        compiler_params=pltpu.CompilerParams(
            collective_id=1, has_side_effects=True, vmem_limit_bytes=VMEM_LIMIT
        ),
        name="close",
    )(length, terms.reshape(shape), own, gate_rows)


def local(
    input_activations,
    prompt_extents,
    continuing_flags,
    owning_index,
    partition_arrangement,
    training_accept_pieces,
    training_lookup_pieces,
    training_content_pieces,
    normalizer_scales,
    prior_step_blends,
    forgetting_bias_vector,
    forgetting_left_lowrank,
    forgetting_right_lowrank,
    instant_emphasis,
    group_normalizer_scale,
    gating_projection,
    mixing_exit_projection,
    kept_summary_places,
    previous_normed_entries,
    feedforward_entry_proj,
    feedforward_exit_proj,
    feedforward_accept_proj,
):
    x = input_activations[0]
    rows, width = x.shape
    lw = mixing_exit_projection.shape[0]
    hid = lax.axis_size("hid")
    block_rows = training_accept_pieces.shape[0]
    w, s0, mate, rest, before, after = spread(
        owning_index, continuing_flags, training_accept_pieces, training_lookup_pieces,
        training_content_pieces, kept_summary_places[0, 0], feedforward_entry_proj,
        feedforward_exit_proj, hid,
    )
    before_mate, after_mate = send(mate, 1, 0), send(mate, NX - 1, 0)
    w = w.reshape(-1, 3 * block_rows, lw)
    terms, state, last_in, x_share = time_mix(
        partition_arrangement, prompt_extents, continuing_flags, x, previous_normed_entries[0],
        normalizer_scales, prior_step_blends,
        gating_projection, forgetting_left_lowrank, forgetting_right_lowrank,
        forgetting_bias_vector[None], instant_emphasis[None], group_normalizer_scale[None],
        s0, mixing_exit_projection, w,
    )
    middle, own_middle, far, far_mate, before_rest, after_rest, far_rest = join(
        terms, x_share, before, after_mate, rest
    )
    out_terms, gate_rows, shift_out = channel_mix(
        prompt_extents, continuing_flags, last_in, middle.reshape(hid, rows, lw),
        previous_normed_entries[0], normalizer_scales, prior_step_blends, feedforward_accept_proj,
        [feedforward_entry_proj, feedforward_exit_proj, before, after, far]
        + [mate, before_mate, after_mate, far_mate, rest, before_rest, after_rest, far_rest],
    )
    layer_out = close(prompt_extents, out_terms, own_middle, gate_rows)[None]
    return (layer_out, state[None], shift_out[None])


def solution(mesh):
    placed = (
        P("req", None, None),
        P("req"),
        P("req"),
        P("req"),
        P(),
        P(("req", "hid"), None),
        P(("req", "hid"), None),
        P(("req", "hid"), None),
        P(),
        P(),
        P("hid"),
        P(),
        P(None, "hid"),
        P("hid"),
        P("hid"),
        P(None, "hid"),
        P("hid", None),
        P("req", "hid", None, None, None),
        P("req", None, None),
        P(("req", "hid"), None),
        P(("req", "hid"), None),
        P(None, "hid"),
    )
    return jax.shard_map(
        local,
        mesh=mesh,
        in_specs=placed,
        out_specs=(P("req", None, "hid"), P("req", "hid", None, None), P("req", None, None)),
        check_vma=False,
    )
```
